128 devices in a mesh: row: 2 (over x_hi), col: 4 (over x_lo, core), layer: 16 (over z, y).
Axes of the slice: x: 4 (x_hi: 2, x_lo: 2; x = x_hi * 2 + x_lo), y: 4, z: 4, core: 2. Of those that a mesh axis runs over, the one named last changes fastest.
Arguments:
- front: float32 [8192, 8192], P('row', ('col', 'layer')), may hold values from -8 to 256, as said below
Outputs:
- eliminated: float32 [8192, 8192], P('row', ('col', 'layer'))
The draws below stay inside these ranges and needn't reach their ends.
Inputs may be any that keep to these rules, and one draw needn't show every extreme that they name: `front`: every pivot block met during the elimination has a nonzero diagonal, and the Newton-Schulz iteration started from the inverse of its diagonal converges.
All inputs are finite; a program needn't handle non-finite values.
Results may differ from the reference program's by a relative error of at most 0.0001.
Values sent between devices are 32-bit elements; how exact they have to be, the bound alone decides.
No kernel may reach another device: no remote copies, remote signals or barrier semaphores. Data moves between devices by JAX's collectives and lax.ppermute only.
A program may use at most 64 MiB of HBM per device.

```python
import jax
import jax.numpy as jnp
from jax import lax

M = 8192
B = 64
ITERS = 2
P_SIZE = 256


def draw_front(key, part):
    normal_key, diag_key = jax.random.split(jax.random.fold_in(key, 17), 2)
    scatter = jnp.clip(jax.random.normal(normal_key, (M, M), jnp.float32), -5.0, 5.0)
    leading = jax.random.uniform(diag_key, (M,), jnp.float32, 32.0, 64.0)
    places = jnp.arange(M)
    matrix = scatter.at[places, places].set(leading)
    return matrix


def setup_inputs(seed: int = 0) -> dict:
    seeds = jax.random.split(jax.random.key(seed), 2)
    return {
        "front": draw_front(jax.random.fold_in(seeds[1], 71), 0),
    }


def exact_dot(left, right):
    return jnp.dot(left, right, precision=lax.Precision.HIGHEST, preferred_element_type=jnp.float32)


def newton_inverse(pivot):
    inverse = jnp.diag(1.0 / jnp.diagonal(pivot))
    for sweep in range(ITERS):
        inverse = 2.0 * inverse - exact_dot(inverse, exact_dot(pivot, inverse))
    return inverse


def reference(front):
    matrix = front.astype(jnp.float32)
    for block in range(P_SIZE // B):
        block_begin = block * B
        block_end = block_begin + B
        pivot = matrix[block_begin:block_end, block_begin:block_end]
        inverse = newton_inverse(pivot)
        lower = exact_dot(matrix[block_end:, block_begin:block_end], inverse)
        upper = matrix[block_begin:block_end, block_end:]
        matrix = matrix.at[block_end:, block_end:].add(-exact_dot(lower, upper))
        matrix = matrix.at[block_end:, block_begin:block_end].set(lower)
    return matrix
```

```python
import jax
import jax.numpy as jnp
import numpy as np
from jax import lax
from jax.experimental import pallas as pl
from jax.experimental.pallas import tpu as pltpu
from jax.sharding import PartitionSpec as P

B = 64
ITERS = 2
P_SIZE = 256

AXES = ("row", "x", "core", "z", "y")
SHAPE = (2, 2, 2, 4, 4)
ROWS = 4096
WIDTH = 128
SHARE = 512
DPART = 128


def place(r, x, c, z, y):
    return (((r * 2 + x) * 2 + c) * 4 + z % 4) * 4 + y % 4


def everywhere(zy_pairs, xs=(0, 1)):
    return [
        (place(r, x, c, *a), place(r, x, c, *b)) for r in range(2) for x in xs for c in range(2) for a, b in zy_pairs
    ]


ALL_ZY = [(z, y) for z in range(4) for y in range(4)]


def shift(dz, dy):
    return everywhere([((z, y), (z + dz, y + dy)) for z, y in ALL_ZY])


ROW_DOWN = [(place(0, x, c, z, y), place(1, x, c, z, y)) for x in range(2) for c in range(2) for z, y in ALL_ZY]
CORE_SWAP = [
    (place(r, x, c, z, y), place(r, x, 1 - c, z, y)) for r in range(2) for x in range(2) for c in range(2) for z, y in ALL_ZY
]
X_SWAP = [
    (place(r, x, c, z, y), place(r, 1 - x, c, z, y)) for r in range(2) for x in range(2) for c in range(2) for z, y in ALL_ZY
]


def coset(z, y):
    return (z + 2 * y) % 4


HOLDERS = (
    {0: (0, 0), 1: (1, 0), 3: (3, 0), 2: (0, 3)},
    {2: (0, 1), 3: (1, 1), 1: (3, 1), 0: (0, 2)},
)
TO_UP = everywhere([((0, 0), (1, 0)), ((0, 1), (1, 1))], xs=(0,))
TO_DOWN = everywhere([((0, 0), (3, 0)), ((0, 1), (3, 1))], xs=(0,))
TO_SIDE = everywhere([((0, 0), (0, 3)), ((0, 1), (0, 2))], xs=(0,))
ROLE = np.zeros((16,), np.int32)
SWAP_PAIRS, FIRST_PAIRS, SECOND_PAIRS = [], [], []
for _c in range(4):
    _m0, _m1 = HOLDERS[0][_c], HOLDERS[1][_c]
    _m2, _m3 = [m for m in ALL_ZY if coset(*m) == _c and m not in (_m0, _m1)]
    for _role, _m in enumerate((_m0, _m1, _m2, _m3)):
        ROLE[_m[0] * 4 + _m[1]] = _role
    SWAP_PAIRS += [(_m0, _m1), (_m1, _m0)]
    FIRST_PAIRS += [(_m0, _m2), (_m1, _m3)]
    SECOND_PAIRS += [(_m0, _m3), (_m1, _m2)]
SWAP_PAIRS, FIRST_PAIRS, SECOND_PAIRS = map(everywhere, (SWAP_PAIRS, FIRST_PAIRS, SECOND_PAIRS))


def send(value, pairs):
    return lax.ppermute(value, AXES, pairs)


def exact_dot(left, right):
    return jnp.dot(left, right, precision=lax.Precision.HIGHEST, preferred_element_type=jnp.float32)


def factor_kernel(info, d_mine, d_other, top, update_out, top_out, f):
    core, panel, second = info[0], info[1], info[2]
    for half in range(2):
        @pl.when(core == half)
        def _():
            for part in range(2):
                f[half * DPART : (half + 1) * DPART, part * WIDTH : (part + 1) * WIDTH] = d_mine[part]
                f[(1 - half) * DPART : (2 - half) * DPART, part * WIDTH : (part + 1) * WIDTH] = d_other[part]

    f[0:P_SIZE, P_SIZE:] = top[...]
    rows = lax.broadcasted_iota(jnp.int32, (P_SIZE, P_SIZE), 0)
    cols = lax.broadcasted_iota(jnp.int32, (P_SIZE, P_SIZE), 1)
    f[P_SIZE:, 0:P_SIZE] = jnp.where(rows == cols, 1.0, 0.0)
    f[P_SIZE:, P_SIZE:] = jnp.zeros((P_SIZE, WIDTH), jnp.float32)
    total = P_SIZE + WIDTH
    for block in range(P_SIZE // B):
        lo, hi = block * B, block * B + B
        base = lo // WIDTH * WIDTH
        r = lax.broadcasted_iota(jnp.int32, (WIDTH, WIDTH), 0) + base
        c = lax.broadcasted_iota(jnp.int32, (WIDTH, WIDTH), 1) + base
        in_block = (r >= lo) & (r < hi) & (c >= lo) & (c < hi)
        on_diag = in_block & (r == c)
        window = f[base : base + WIDTH, base : base + WIDTH]
        pivot = jnp.where(in_block, window, 0.0)
        diag = jnp.where(on_diag, window, 0.0)
        diag_row = jnp.sum(diag, axis=0, keepdims=True)
        diag_col = jnp.sum(diag, axis=1, keepdims=True)
        inv_row = 1.0 / jnp.where(diag_row == 0.0, 1.0, diag_row)
        inv_col = 1.0 / jnp.where(diag_col == 0.0, 1.0, diag_col)
        inverse = jnp.where(on_diag, 2.0 * inv_row, 0.0) - inv_col * (pivot * inv_row)
        for _ in range(ITERS - 1):
            inverse = 2.0 * inverse - exact_dot(inverse, exact_dot(pivot, inverse))
        lower = exact_dot(f[hi:, base : base + WIDTH], inverse)
        col = lax.broadcasted_iota(jnp.int32, (WIDTH, total), 1)
        upper = jnp.where(col >= hi, f[base : base + WIDTH, :], 0.0)
        f[hi:, :] = f[hi:, :] - exact_dot(lower, upper)
        lane = lax.broadcasted_iota(jnp.int32, lower.shape, 1) + base
        mine = (lane >= lo) & (lane < hi)
        f[hi:, base : base + WIDTH] = jnp.where(mine, lower, f[hi:, base : base + WIDTH])

    @pl.when(panel == 0)
    def _():
        update_out[...] = f[P_SIZE:, P_SIZE:]
        top_out[...] = f[0:P_SIZE, P_SIZE:]

    for part in range(2):
        @pl.when((panel == 1) & (second == part))
        def _():
            update_out[...] = f[P_SIZE:, part * WIDTH : (part + 1) * WIDTH]
            top_out[...] = f[0:P_SIZE, part * WIDTH : (part + 1) * WIDTH]


def factor(info, d_mine, d_other, top):
    vmem = pl.BlockSpec(memory_space=pltpu.VMEM)
    out = jax.ShapeDtypeStruct((P_SIZE, WIDTH), jnp.float32)
    return pl.pallas_call(
        factor_kernel,
        out_shape=(out, out),
        in_specs=[pl.BlockSpec(memory_space=pltpu.SMEM), vmem, vmem, vmem],
        out_specs=(vmem, vmem),
        scratch_shapes=[pltpu.VMEM((2 * P_SIZE, P_SIZE + WIDTH), jnp.float32)],
        name="factor",
    )(info, d_mine, d_other, top)


def update_body(places, info, front, parts, update, top, out):
    step = pl.program_id(0)
    keep = jnp.where(info[1] == 0, front[...], 0.0)
    first, second = update[0:WIDTH, :], update[WIDTH:, :]
    for at, part in enumerate(parts[:3]):
        @pl.when(step == at)
        def _():
            out[...] = keep + (exact_dot(part[0], first) + exact_dot(part[1], second))

    @pl.when(step == 3)
    def _():
        for half, part in enumerate(parts[3:]):
            rows = slice(half * (SHARE // 2), (half + 1) * (SHARE // 2))
            out[rows, :] = keep[rows, :] + (exact_dot(part[0], first) + exact_dot(part[1], second))

    @pl.when((places[step] == 0) & (info[3] == 0))
    def _():
        out[0:P_SIZE, :] = top[...]


def first_update_kernel(places, info, front, p0, p1, p2, p3, p4, update, top, out):
    update_body(places, info, front, (p0, p1, p2, p3, p4), update, top, out)


def second_update_kernel(places, info, front, p0, p1, p2, p3, p4, update, top, _, out):
    update_body(places, info, front, (p0, p1, p2, p3, p4), update, top, out)


def apply_update(places, info, front, parts, update, top, done=None):
    vmem = pl.BlockSpec(memory_space=pltpu.VMEM)
    block = pl.BlockSpec((SHARE, WIDTH), lambda i, places, info: (places[i], 0))
    more = [] if done is None else [pl.BlockSpec(memory_space=pl.ANY)]
    extra = [] if done is None else [done]
    return pl.pallas_call(
        first_update_kernel if done is None else second_update_kernel,
        out_shape=jax.ShapeDtypeStruct((ROWS, WIDTH), jnp.float32),
        grid_spec=pltpu.PrefetchScalarGridSpec(
            num_scalar_prefetch=2,
            grid=(4,),
            in_specs=[block] + [vmem] * 7 + more,
            out_specs=block,
        ),
        input_output_aliases={} if done is None else {10: 0},
        name="update_mine" if done is None else "update_other",
    )(places, info, front, *parts, update, top, *extra)


def per_device(front):
    row, x, core, z, y = (lax.axis_index(a) for a in AXES)
    mine = coset(z, y)
    source = (x == 0) & (z == 0) & (y < 2)
    panel = source & (core == 0)
    info = jnp.stack([core, panel.astype(jnp.int32), y, row]).astype(jnp.int32)

    top_own = front[:P_SIZE]
    top_down = send(top_own, ROW_DOWN)
    half_other = send(front[ROWS // 2 :], CORE_SWAP)
    top = jnp.where(row == 0, top_own, top_down)
    d_swapped = send(top[DPART:], CORE_SWAP)
    half = jnp.where(core == 0, front[: ROWS // 2], half_other)
    d_part = jnp.where(core == 0, top[:DPART], d_swapped)

    def share(delta):
        start = (mine + delta) % 4 * SHARE
        return jnp.concatenate([d_part, lax.dynamic_slice(half, (start, 0), (SHARE, WIDTH))])

    up = send(share(1), TO_UP)
    down = send(share(3), TO_DOWN)
    side = send(share(2), TO_SIDE)
    held = jnp.where(source, share(0), up + down + side)
    held = jnp.where(x == 0, held, send(held, X_SWAP))

    swapped = send(held, SWAP_PAIRS)
    first = send(held, FIRST_PAIRS)
    second = send(held, SECOND_PAIRS)
    role = jnp.asarray(ROLE)[z * 4 + y]

    def pick(a, b, c, d):
        return jnp.where(role == 0, a, jnp.where(role == 1, b, jnp.where(role == 2, c, d)))

    left = pick(held, swapped, first, second)
    right = pick(swapped, held, second, first)
    own = jnp.stack([left[DPART:], right[DPART:]])
    d_mine = jnp.stack([left[:DPART], right[:DPART]])
    d_other = send(d_mine, CORE_SWAP)

    before = send(own, shift(1, 0))
    after = send(own, shift(-1, 0))
    far_low = send(own[:, : SHARE // 2], shift(0, 1))
    far_high = send(own[:, SHARE // 2 :], shift(0, -1))
    own_other = send(own, CORE_SWAP)
    update, top_done = factor(info, d_mine, d_other, top)

    received = (before, after, far_low, far_high)
    others = tuple(send(v, CORE_SWAP) for v in received)
    order = jnp.stack([mine, (mine + 3) % 4, (mine + 1) % 4, (mine + 2) % 4]).astype(jnp.int32)
    out = apply_update(order + core * 4, info, front, (own, *received), update, top_done)
    return apply_update(order + (1 - core) * 4, info, front, (own_other, *others), update, top_done, out)


def solution(mesh):
    wide = jax.sharding.Mesh(mesh.devices.reshape(SHAPE), AXES)
    spec = P("row", ("x", "core", "z", "y"))
    return jax.shard_map(per_device, mesh=wide, in_specs=(spec,), out_specs=spec, check_vma=False)
```

```python
import jax
import jax.numpy as jnp
import numpy as np
from jax import lax
from jax.experimental import pallas as pl
from jax.experimental.pallas import tpu as pltpu
from jax.sharding import PartitionSpec as P

B = 64
ITERS = 2
P_SIZE = 256

AXES = ("row", "x", "core", "z", "y")
SHAPE = (2, 2, 2, 4, 4)
ROWS = 4096
WIDTH = 128
SHARE = 512
DPART = 128


def place(r, x, c, z, y):
    return (((r * 2 + x) * 2 + c) * 4 + z % 4) * 4 + y % 4


def everywhere(zy_pairs, xs=(0, 1)):
    return [
        (place(r, x, c, *a), place(r, x, c, *b)) for r in range(2) for x in xs for c in range(2) for a, b in zy_pairs
    ]


ALL_ZY = [(z, y) for z in range(4) for y in range(4)]


def shift(dz, dy):
    return everywhere([((z, y), (z + dz, y + dy)) for z, y in ALL_ZY])


ROW_DOWN = [(place(0, x, c, z, y), place(1, x, c, z, y)) for x in range(2) for c in range(2) for z, y in ALL_ZY]
CORE_SWAP = [
    (place(r, x, c, z, y), place(r, x, 1 - c, z, y)) for r in range(2) for x in range(2) for c in range(2) for z, y in ALL_ZY
]
X_SWAP = [
    (place(r, x, c, z, y), place(r, 1 - x, c, z, y)) for r in range(2) for x in range(2) for c in range(2) for z, y in ALL_ZY
]


def coset(z, y):
    return (z + 2 * y) % 4


SIDE = everywhere([((z, y), (z, 3 - y)) for z, y in ALL_ZY])
ROW_SWAP = ROW_DOWN + [(b, a) for a, b in ROW_DOWN]


def member(z, y):
    near = ((y == 0) & (z != 2)) | ((y == 3) & (z == 0))
    far = ((y == 1) & (z != 2)) | ((y == 2) & (z == 0))
    third = ((z == 2) & (y < 2)) | ((z == 1) & (y >= 2))
    return jnp.where(near, 0, jnp.where(far, 1, jnp.where(third, 2, 3)))


def flipped(z, y):
    return member(z % 4, y % 4) % 2


def member_pairs():
    swap, first, second = [], [], []
    for c in range(4):
        m = {}
        for z, y in ALL_ZY:
            near = (y == 0 and z != 2) or (z, y) == (0, 3)
            far = (y == 1 and z != 2) or (z, y) == (0, 2)
            third = (z == 2 and y < 2) or (z == 1 and y >= 2)
            if coset(z, y) == c:
                m[0 if near else 1 if far else 2 if third else 3] = (z, y)
        swap += [(m[0], m[1]), (m[1], m[0])]
        first += [(m[0], m[2]), (m[1], m[3])]
        second += [(m[0], m[3]), (m[1], m[2])]
    return everywhere(swap), everywhere(first), everywhere(second)


SWAP_PAIRS, FIRST_PAIRS, SECOND_PAIRS = member_pairs()


def send(value, pairs):
    return lax.ppermute(value, AXES, pairs)


def exact_dot(left, right):
    return jnp.dot(left, right, precision=lax.Precision.HIGHEST, preferred_element_type=jnp.float32)


def factor_kernel(info, d_mine, d_other, top, update_out, top_out, f):
    core, panel, second = info[0], info[1], info[2]
    for half in range(2):
        @pl.when(core == half)
        def _():
            for part in range(2):
                f[half * DPART : (half + 1) * DPART, part * WIDTH : (part + 1) * WIDTH] = d_mine[part]
                f[(1 - half) * DPART : (2 - half) * DPART, part * WIDTH : (part + 1) * WIDTH] = d_other[part]

    f[0:P_SIZE, P_SIZE:] = top[...]
    rows = lax.broadcasted_iota(jnp.int32, (P_SIZE, P_SIZE), 0)
    cols = lax.broadcasted_iota(jnp.int32, (P_SIZE, P_SIZE), 1)
    f[P_SIZE:, 0:P_SIZE] = jnp.where(rows == cols, 1.0, 0.0)
    f[P_SIZE:, P_SIZE:] = jnp.zeros((P_SIZE, WIDTH), jnp.float32)
    total = P_SIZE + WIDTH
    for block in range(P_SIZE // B):
        lo, hi = block * B, block * B + B
        base = lo // WIDTH * WIDTH
        r = lax.broadcasted_iota(jnp.int32, (WIDTH, WIDTH), 0) + base
        c = lax.broadcasted_iota(jnp.int32, (WIDTH, WIDTH), 1) + base
        in_block = (r >= lo) & (r < hi) & (c >= lo) & (c < hi)
        on_diag = in_block & (r == c)
        window = f[base : base + WIDTH, base : base + WIDTH]
        pivot = jnp.where(in_block, window, 0.0)
        diag = jnp.where(on_diag, window, 0.0)
        diag_row = jnp.sum(diag, axis=0, keepdims=True)
        diag_col = jnp.sum(diag, axis=1, keepdims=True)
        inv_row = 1.0 / jnp.where(diag_row == 0.0, 1.0, diag_row)
        inv_col = 1.0 / jnp.where(diag_col == 0.0, 1.0, diag_col)
        inverse = jnp.where(on_diag, 2.0 * inv_row, 0.0) - inv_col * (pivot * inv_row)
        for _ in range(ITERS - 1):
            inverse = 2.0 * inverse - exact_dot(inverse, exact_dot(pivot, inverse))
        lower = exact_dot(f[hi:, base : base + WIDTH], inverse)
        col = lax.broadcasted_iota(jnp.int32, (WIDTH, total), 1)
        upper = jnp.where(col >= hi, f[base : base + WIDTH, :], 0.0)
        f[hi:, :] = f[hi:, :] - exact_dot(lower, upper)
        lane = lax.broadcasted_iota(jnp.int32, lower.shape, 1) + base
        mine = (lane >= lo) & (lane < hi)
        f[hi:, base : base + WIDTH] = jnp.where(mine, lower, f[hi:, base : base + WIDTH])

    def finish(update, done):
        high = update.astype(jnp.bfloat16)
        low = (update - high.astype(jnp.float32)).astype(jnp.bfloat16)
        both = jnp.concatenate([high, low], axis=1)
        update_out[0] = both
        update_out[1] = jnp.concatenate([both[WIDTH:], both[:WIDTH]], axis=0)
        top_out[...] = done

    @pl.when(panel == 0)
    def _():
        finish(f[P_SIZE:, P_SIZE:], f[0:P_SIZE, P_SIZE:])

    for part in range(2):
        @pl.when((panel == 1) & (second == part))
        def _():
            side = slice(part * WIDTH, (part + 1) * WIDTH)
            finish(f[P_SIZE:, side], f[0:P_SIZE, side])


def factor(info, d_mine, d_other, top):
    vmem = pl.BlockSpec(memory_space=pltpu.VMEM)
    return pl.pallas_call(
        factor_kernel,
        out_shape=(
            jax.ShapeDtypeStruct((2, P_SIZE, 2 * WIDTH), jnp.bfloat16),
            jax.ShapeDtypeStruct((P_SIZE, WIDTH), jnp.float32),
        ),
        in_specs=[pl.BlockSpec(memory_space=pltpu.SMEM), vmem, vmem, vmem],
        out_specs=(vmem, vmem),
        scratch_shapes=[pltpu.VMEM((2 * P_SIZE, P_SIZE + WIDTH), jnp.float32)],
        cost_estimate=pl.CostEstimate(flops=9_000_000_000, bytes_accessed=2_000_000, transcendentals=0),
        name="factor",
    )(info, d_mine, d_other, top)


def update_body(places, info, front, parts, update, top, out):
    step = pl.program_id(0)
    for at in range(4):
        @pl.when(step == at)
        def _():
            rows = jnp.concatenate([parts[2 * at][...], parts[2 * at + 1][...]], axis=1)
            high = rows.astype(jnp.bfloat16)
            low = (rows - high.astype(jnp.float32)).astype(jnp.bfloat16)
            factor_rows = update[places[4 + at]]
            both = jnp.dot(high, factor_rows, preferred_element_type=jnp.float32)
            both = both + jnp.dot(low, factor_rows, preferred_element_type=jnp.float32)
            out[...] = jnp.where(info[1] == 0, front[...], 0.0) + (both[:, :WIDTH] + both[:, WIDTH:])

    @pl.when((places[step] == 0) & (info[3] == 0))
    def _():
        out[0:P_SIZE, :] = top[...]


def first_update_kernel(places, info, front, p0, p1, p2, p3, p4, p5, p6, p7, update, top, out):
    update_body(places, info, front, (p0, p1, p2, p3, p4, p5, p6, p7), update, top, out)


def second_update_kernel(places, info, front, p0, p1, p2, p3, p4, p5, p6, p7, update, top, _, out):
    update_body(places, info, front, (p0, p1, p2, p3, p4, p5, p6, p7), update, top, out)


def apply_update(places, info, front, parts, update, top, done=None):
    vmem = pl.BlockSpec(memory_space=pltpu.VMEM)
    block = pl.BlockSpec((SHARE, WIDTH), lambda i, places, info: (places[i], 0))
    more = [] if done is None else [pl.BlockSpec(memory_space=pl.ANY)]
    extra = [] if done is None else [done]
    return pl.pallas_call(
        first_update_kernel if done is None else second_update_kernel,
        out_shape=jax.ShapeDtypeStruct((ROWS, WIDTH), jnp.float32),
        grid_spec=pltpu.PrefetchScalarGridSpec(
            num_scalar_prefetch=2,
            grid=(4,),
            in_specs=[block] + [vmem] * 10 + more,
            out_specs=block,
        ),
        input_output_aliases={} if done is None else {13: 0},
        cost_estimate=pl.CostEstimate(flops=3_000_000_000, bytes_accessed=4_000_000, transcendentals=0),
        name="update_mine" if done is None else "update_other",
    )(places, info, front, *parts, update, top, *extra)


def per_device(front):
    row, x, core, z, y = (lax.axis_index(a) for a in AXES)
    mine = coset(z, y)
    panel = (x == 0) & (z == 0) & (y < 2) & (core == 0)
    info = jnp.stack([core, panel.astype(jnp.int32), y, row]).astype(jnp.int32)

    d_part = jnp.where(core == 0, front[:DPART], send(front[DPART:P_SIZE], CORE_SWAP))

    def share(delta):
        start = (mine + delta) % 4 * SHARE
        kept = lax.dynamic_slice(front, (start, 0), (SHARE, WIDTH))
        given = lax.dynamic_slice(front, (start + ROWS // 2, 0), (SHARE, WIDTH))
        return jnp.concatenate([d_part, jnp.where(core == 0, kept, send(given, CORE_SWAP))])

    up = send(share(1), shift(1, 0))
    down = send(share(3), shift(-1, 0))
    side = send(share(2), SIDE)
    top_swapped = send(front[:P_SIZE], ROW_SWAP)
    top = jnp.where(row == 0, front[:P_SIZE], top_swapped)
    near = y < 2
    held = jnp.where((z == 1) & near, up, jnp.where((z == 3) & near, down, jnp.where(near, share(0), side)))
    held_share = held[DPART:]
    held_share = jnp.where(x == 0, held_share, send(held_share, X_SWAP))
    held_d = jnp.where(row == 0, held[:DPART], send(held[:DPART], ROW_SWAP))
    held_d = jnp.where(x == 0, held_d, send(held_d, X_SWAP))
    held = jnp.concatenate([held_d, held_share])

    to_first = send(held, FIRST_PAIRS)
    swapped = send(held, SWAP_PAIRS)
    to_second = send(held, SECOND_PAIRS)
    holder = member(z, y) < 2
    flip = flipped(z, y)
    part0 = jnp.where(holder, held, to_first)
    part1 = jnp.where(holder, swapped, to_second)
    own0, own1 = part0[DPART:], part1[DPART:]
    before0 = send(own0, shift(1, 0))
    after0 = send(own0, shift(-1, 0))
    d_mine = jnp.where(flip == 0, jnp.stack([part0[:DPART], part1[:DPART]]), jnp.stack([part1[:DPART], part0[:DPART]]))
    d_other = send(d_mine, CORE_SWAP)
    left = jnp.where(flip == 0, own0, own1)
    right = jnp.where(flip == 0, own1, own0)
    before1 = send(own1, shift(1, 0))
    after1 = send(own1, shift(-1, 0))
    far0 = send(left, shift(0, 1))
    far1 = send(right, shift(0, -1))
    update, top_done = factor(info, d_mine, d_other, top)

    parts = (own0, own1, before0, before1, after0, after1, far0, far1)
    others = tuple(send(v, CORE_SWAP) for v in parts)
    order = [mine, (mine + 3) % 4, (mine + 1) % 4, (mine + 2) % 4]
    flips = [flip, flipped(z - 1, y), flipped(z + 1, y), jnp.zeros_like(flip)]
    places = [jnp.stack([p + 4 * c for p in order] + flips).astype(jnp.int32) for c in (core, 1 - core)]
    out = apply_update(places[0], info, front, parts, update, top_done)
    return apply_update(places[1], info, front, others, update, top_done, out)


def solution(mesh):
    wide = jax.sharding.Mesh(mesh.devices.reshape(SHAPE), AXES)
    spec = P("row", ("x", "core", "z", "y"))
    return jax.shard_map(per_device, mesh=wide, in_specs=(spec,), out_specs=spec, check_vma=False)
```

```python
import jax
import jax.numpy as jnp
from jax import lax
from jax.experimental import pallas as pl
from jax.experimental.pallas import tpu as pltpu
from jax.sharding import PartitionSpec as P


B = 64
ITERS = 2
P_SIZE = 256

AXES = ("row", "x", "core", "z", "y")
SHAPE = (2, 2, 2, 4, 4)
ROWS = 4096
WIDTH = 128
SHARE = 512
DPART = 128


def place(r, x, c, z, y):
    return (((r * 2 + x) * 2 + c) * 4 + z % 4) * 4 + y % 4


def everywhere(zy_pairs, xs=(0, 1)):
    return [
        (place(r, x, c, *a), place(r, x, c, *b)) for r in range(2) for x in xs for c in range(2) for a, b in zy_pairs
    ]


ALL_ZY = [(z, y) for z in range(4) for y in range(4)]


def shift(dz, dy):
    return everywhere([((z, y), (z + dz, y + dy)) for z, y in ALL_ZY])


ROW_DOWN = [(place(0, x, c, z, y), place(1, x, c, z, y)) for x in range(2) for c in range(2) for z, y in ALL_ZY]
CORE_SWAP = [
    (place(r, x, c, z, y), place(r, x, 1 - c, z, y)) for r in range(2) for x in range(2) for c in range(2) for z, y in ALL_ZY
]
X_SWAP = [
    (place(r, x, c, z, y), place(r, 1 - x, c, z, y)) for r in range(2) for x in range(2) for c in range(2) for z, y in ALL_ZY
]


def coset(z, y):
    return (z + 2 * y) % 4


SIDE = everywhere([((z, y), (z, 3 - y)) for z, y in ALL_ZY])
ROW_SWAP = ROW_DOWN + [(b, a) for a, b in ROW_DOWN]


def member(z, y):
    near = ((y == 0) & (z != 2)) | ((y == 3) & (z == 0))
    far = ((y == 1) & (z != 2)) | ((y == 2) & (z == 0))
    third = ((z == 2) & (y < 2)) | ((z == 1) & (y >= 2))
    return jnp.where(near, 0, jnp.where(far, 1, jnp.where(third, 2, 3)))


def member_pairs():
    swap, first, second = [], [], []
    for c in range(4):
        m = {}
        for z, y in ALL_ZY:
            near = (y == 0 and z != 2) or (z, y) == (0, 3)
            far = (y == 1 and z != 2) or (z, y) == (0, 2)
            third = (z == 2 and y < 2) or (z == 1 and y >= 2)
            if coset(z, y) == c:
                m[0 if near else 1 if far else 2 if third else 3] = (z, y)
        swap += [(m[0], m[1]), (m[1], m[0])]
        first += [(m[0], m[2]), (m[1], m[3])]
        second += [(m[0], m[3]), (m[1], m[2])]
    return everywhere(swap), everywhere(first), everywhere(second)


SWAP_PAIRS, FIRST_PAIRS, SECOND_PAIRS = member_pairs()


def send(value, pairs):
    return lax.ppermute(value, AXES, pairs)


def in_vmem(value):
    return pltpu.with_memory_space_constraint(value, pltpu.VMEM)


def exact_dot(left, right):
    return jnp.dot(left, right, precision=lax.Precision.HIGHEST, preferred_element_type=jnp.float32)


def factor_kernel(info, d_mine, d_other, top, update_out, top_out, f):
    core, panel, second = info[0], info[1], info[2]
    for half in range(2):
        @pl.when(core == half)
        def _():
            for part in range(2):
                f[half * DPART : (half + 1) * DPART, part * WIDTH : (part + 1) * WIDTH] = d_mine[part]
                f[(1 - half) * DPART : (2 - half) * DPART, part * WIDTH : (part + 1) * WIDTH] = d_other[part]

    f[0:P_SIZE, P_SIZE:] = top[...]
    rows = lax.broadcasted_iota(jnp.int32, (P_SIZE, P_SIZE), 0)
    cols = lax.broadcasted_iota(jnp.int32, (P_SIZE, P_SIZE), 1)
    f[P_SIZE:, 0:P_SIZE] = jnp.where(rows == cols, 1.0, 0.0)
    f[P_SIZE:, P_SIZE:] = jnp.zeros((P_SIZE, WIDTH), jnp.float32)
    total = P_SIZE + WIDTH
    for block in range(P_SIZE // B):
        lo, hi = block * B, block * B + B
        base = lo // WIDTH * WIDTH
        r = lax.broadcasted_iota(jnp.int32, (WIDTH, WIDTH), 0) + base
        c = lax.broadcasted_iota(jnp.int32, (WIDTH, WIDTH), 1) + base
        in_block = (r >= lo) & (r < hi) & (c >= lo) & (c < hi)
        on_diag = in_block & (r == c)
        window = f[base : base + WIDTH, base : base + WIDTH]
        pivot = jnp.where(in_block, window, 0.0)
        diag = jnp.where(on_diag, window, 0.0)
        diag_row = jnp.sum(diag, axis=0, keepdims=True)
        diag_col = jnp.sum(diag, axis=1, keepdims=True)
        inv_row = 1.0 / jnp.where(diag_row == 0.0, 1.0, diag_row)
        inv_col = 1.0 / jnp.where(diag_col == 0.0, 1.0, diag_col)
        inverse = jnp.where(on_diag, 2.0 * inv_row, 0.0) - inv_col * (pivot * inv_row)
        for _ in range(ITERS - 1):
            inverse = 2.0 * inverse - exact_dot(inverse, exact_dot(pivot, inverse))
        lower = exact_dot(f[hi:, base : base + WIDTH], inverse)
        col = lax.broadcasted_iota(jnp.int32, (WIDTH, total), 1)
        upper = jnp.where(col >= hi, f[base : base + WIDTH, :], 0.0)
        f[hi:, :] = f[hi:, :] - exact_dot(lower, upper)
        lane = lax.broadcasted_iota(jnp.int32, lower.shape, 1) + base
        mine = (lane >= lo) & (lane < hi)
        f[hi:, base : base + WIDTH] = jnp.where(mine, lower, f[hi:, base : base + WIDTH])

    def finish(update, done):
        high = update.astype(jnp.bfloat16)
        low = (update - high.astype(jnp.float32)).astype(jnp.bfloat16)
        update_out[...] = jnp.concatenate([high, low], axis=1)
        top_out[...] = done

    @pl.when(panel == 0)
    def _():
        finish(f[P_SIZE:, P_SIZE:], f[0:P_SIZE, P_SIZE:])

    for part in range(2):
        @pl.when((panel == 1) & (second == part))
        def _():
            side = slice(part * WIDTH, (part + 1) * WIDTH)
            finish(f[P_SIZE:, side], f[0:P_SIZE, side])


def factor(info, d_mine, d_other, top):
    vmem = pl.BlockSpec(memory_space=pltpu.VMEM)
    return pl.pallas_call(
        factor_kernel,
        out_shape=(pltpu.VMEM((P_SIZE, 2 * WIDTH), jnp.bfloat16), pltpu.VMEM((P_SIZE, WIDTH), jnp.float32)),
        in_specs=[pl.BlockSpec(memory_space=pltpu.SMEM), vmem, vmem, vmem],
        out_specs=(vmem, vmem),
        scratch_shapes=[pltpu.VMEM((2 * P_SIZE, P_SIZE + WIDTH), jnp.float32)],
        compiler_params=pltpu.CompilerParams(vmem_limit_bytes=12 << 20),
        cost_estimate=pl.CostEstimate(flops=9_000_000_000, bytes_accessed=2_000_000, transcendentals=0),
        name="factor",
    )(info, in_vmem(d_mine), in_vmem(d_other), in_vmem(top))


def update_body(places, info, front, parts, update, top, out):
    step = pl.program_id(0)

    def rows_of(part, rows):
        panel = jnp.concatenate([part[0], part[1]], axis=1)
        high = panel.astype(jnp.bfloat16)
        low = (panel - high.astype(jnp.float32)).astype(jnp.bfloat16)
        both = jnp.dot(high, update[...], preferred_element_type=jnp.float32)
        both = both + jnp.dot(low, update[...], preferred_element_type=jnp.float32)
        out[rows, :] = jnp.where(info[1] == 0, front[rows, :], 0.0) + (both[:, :WIDTH] + both[:, WIDTH:])

    for at in range(3):
        @pl.when(step == at)
        def _():
            rows_of(parts[at], slice(0, SHARE))

    @pl.when(step == 3)
    def _():
        rows_of(parts[3], slice(0, SHARE // 2))
        rows_of(parts[4], slice(SHARE // 2, SHARE))

    @pl.when((places[step] == 0) & (info[3] == 0))
    def _():
        out[0:P_SIZE, :] = top[...]


def first_update_kernel(places, info, front, p0, p1, p2, p3, p4, update, top, out):
    update_body(places, info, front, (p0, p1, p2, p3, p4), update, top, out)


def second_update_kernel(places, info, front, p0, p1, p2, p3, p4, update, top, _, out):
    update_body(places, info, front, (p0, p1, p2, p3, p4), update, top, out)


def apply_update(places, info, front, parts, update, top, done=None):
    vmem = pl.BlockSpec(memory_space=pltpu.VMEM)
    block = pl.BlockSpec((SHARE, WIDTH), lambda i, places, info: (places[i], 0))
    more = [] if done is None else [pl.BlockSpec(memory_space=pl.ANY)]
    extra = [] if done is None else [done]
    return pl.pallas_call(
        first_update_kernel if done is None else second_update_kernel,
        out_shape=jax.ShapeDtypeStruct((ROWS, WIDTH), jnp.float32),
        grid_spec=pltpu.PrefetchScalarGridSpec(
            num_scalar_prefetch=2,
            grid=(4,),
            in_specs=[block] + [vmem] * 7 + more,
            out_specs=block,
        ),
        input_output_aliases={} if done is None else {10: 0},
        compiler_params=pltpu.CompilerParams(vmem_limit_bytes=12 << 20),
        cost_estimate=pl.CostEstimate(flops=3_000_000_000, bytes_accessed=4_000_000, transcendentals=0),
        name="update_mine" if done is None else "update_other",
    )(places, info, front, *map(in_vmem, parts), in_vmem(update), in_vmem(top), *extra)


def per_device(front):
    row, x, core, z, y = (lax.axis_index(a) for a in AXES)
    mine = coset(z, y)
    panel = (x == 0) & (z == 0) & (y < 2) & (core == 0)
    info = jnp.stack([core, panel.astype(jnp.int32), y, row]).astype(jnp.int32)

    d_part = jnp.where(core == 0, front[:DPART], send(front[DPART:P_SIZE], CORE_SWAP))
    beside = send(front, CORE_SWAP)
    d_part = jnp.where(row == 0, d_part, send(d_part, ROW_SWAP))

    def share(delta):
        start = (mine + delta) % 4 * SHARE
        kept = lax.dynamic_slice(front, (start, 0), (SHARE, WIDTH))
        given = lax.dynamic_slice(beside, (start + ROWS // 2, 0), (SHARE, WIDTH))
        return jnp.concatenate([d_part, jnp.where(core == 0, kept, given)])

    up = send(share(1), shift(1, 0))
    down = send(share(3), shift(-1, 0))
    side = send(share(2), SIDE)
    top_swapped = send(front[:P_SIZE], ROW_SWAP)
    top = jnp.where(row == 0, front[:P_SIZE], top_swapped)
    near = y < 2
    held = jnp.where((z == 1) & near, up, jnp.where((z == 3) & near, down, jnp.where(near, share(0), side)))
    held = jnp.where(x == 0, held, send(held, X_SWAP))

    to_first = send(held, FIRST_PAIRS)
    swapped = send(held, SWAP_PAIRS)
    to_second = send(held, SECOND_PAIRS)
    role = member(z, y)

    def pick(a, b, c, d):
        return jnp.where(role == 0, a, jnp.where(role == 1, b, jnp.where(role == 2, c, d)))

    left = pick(held, swapped, to_first, to_second)
    right = pick(swapped, held, to_second, to_first)
    d_mine = jnp.stack([left[:DPART], right[:DPART]])
    own = jnp.stack([left[DPART:], right[DPART:]])
    d_other = send(d_mine, CORE_SWAP)
    before = send(own, shift(1, 0))
    after = send(own, shift(-1, 0))
    far_low = send(own[:, : SHARE // 2], shift(0, 1))
    far_high = send(own[:, SHARE // 2 :], shift(0, -1))
    own_other = send(own, CORE_SWAP)
    update, top_done = factor(info, d_mine, d_other, top)

    parts = (own, before, after, far_low, far_high)
    others = (own_other, *(send(v, CORE_SWAP) for v in parts[1:]))
    order = [mine, (mine + 3) % 4, (mine + 1) % 4, (mine + 2) % 4]
    places = [jnp.stack([p + 4 * c for p in order]).astype(jnp.int32) for c in (core, 1 - core)]
    out = apply_update(places[0], info, front, parts, update, top_done)
    return apply_update(places[1], info, front, others, update, top_done, out)


def solution(mesh):
    wide = jax.sharding.Mesh(mesh.devices.reshape(SHAPE), AXES)
    spec = P("row", ("x", "core", "z", "y"))

    return jax.shard_map(per_device, mesh=wide, in_specs=(spec,), out_specs=spec, check_vma=False)
```

```python
import jax
import jax.numpy as jnp
from jax import lax
from jax.experimental import pallas as pl
from jax.experimental.pallas import tpu as pltpu
from jax.sharding import PartitionSpec as P


B = 64
ITERS = 2
P_SIZE = 256

AXES = ("row", "x", "core", "z", "y")
SHAPE = (2, 2, 2, 4, 4)
ROWS = 4096
WIDTH = 128
SHARE = 512
DPART = 128


def place(r, x, c, z, y):
    return (((r * 2 + x) * 2 + c) * 4 + z % 4) * 4 + y % 4


def everywhere(zy_pairs, xs=(0, 1)):
    return [
        (place(r, x, c, *a), place(r, x, c, *b)) for r in range(2) for x in xs for c in range(2) for a, b in zy_pairs
    ]


ALL_ZY = [(z, y) for z in range(4) for y in range(4)]


def shift(dz, dy):
    return everywhere([((z, y), (z + dz, y + dy)) for z, y in ALL_ZY])


ROW_DOWN = [(place(0, x, c, z, y), place(1, x, c, z, y)) for x in range(2) for c in range(2) for z, y in ALL_ZY]
CORE_SWAP = [
    (place(r, x, c, z, y), place(r, x, 1 - c, z, y)) for r in range(2) for x in range(2) for c in range(2) for z, y in ALL_ZY
]
X_SWAP = [
    (place(r, x, c, z, y), place(r, 1 - x, c, z, y)) for r in range(2) for x in range(2) for c in range(2) for z, y in ALL_ZY
]


def coset(z, y):
    return (z + 2 * y) % 4


SIDE = everywhere([((z, y), (z, 3 - y)) for z, y in ALL_ZY])
ROW_SWAP = ROW_DOWN + [(b, a) for a, b in ROW_DOWN]


def member(z, y):
    near = ((y == 0) & (z != 2)) | ((y == 3) & (z == 0))
    far = ((y == 1) & (z != 2)) | ((y == 2) & (z == 0))
    third = ((z == 2) & (y < 2)) | ((z == 1) & (y >= 2))
    return jnp.where(near, 0, jnp.where(far, 1, jnp.where(third, 2, 3)))


def member_pairs():
    swap, first, second = [], [], []
    for c in range(4):
        m = {}
        for z, y in ALL_ZY:
            near = (y == 0 and z != 2) or (z, y) == (0, 3)
            far = (y == 1 and z != 2) or (z, y) == (0, 2)
            third = (z == 2 and y < 2) or (z == 1 and y >= 2)
            if coset(z, y) == c:
                m[0 if near else 1 if far else 2 if third else 3] = (z, y)
        swap += [(m[0], m[1]), (m[1], m[0])]
        first += [(m[0], m[2]), (m[1], m[3])]
        second += [(m[0], m[3]), (m[1], m[2])]
    return everywhere(swap), everywhere(first), everywhere(second)


SWAP_PAIRS, FIRST_PAIRS, SECOND_PAIRS = member_pairs()


def send(value, pairs):
    return lax.ppermute(value, AXES, pairs)


def in_vmem(value):
    return pltpu.with_memory_space_constraint(value, pltpu.VMEM)


def split3(value):
    high = value.astype(jnp.bfloat16)
    rest = value - high.astype(jnp.float32)
    middle = rest.astype(jnp.bfloat16)
    low = (rest - middle.astype(jnp.float32)).astype(jnp.bfloat16)
    return high, middle, low


def stacked_dot(left, right):
    lh, lm, ll = split3(left)
    rh, rm, rl = split3(right)
    lefts = jnp.concatenate([ll, lh, lm, lm, lh, lh], axis=1)
    rights = jnp.concatenate([rh, rl, rm, rh, rm, rh], axis=0)
    return jnp.dot(lefts, rights, preferred_element_type=jnp.float32)


def factor_kernel(info, d_mine, d_other, top, update_out, top_out, f):
    core, panel, second = info[0], info[1], info[2]
    for half in range(2):
        @pl.when(core == half)
        def _():
            for part in range(2):
                f[half * DPART : (half + 1) * DPART, part * WIDTH : (part + 1) * WIDTH] = d_mine[part]
                f[(1 - half) * DPART : (2 - half) * DPART, part * WIDTH : (part + 1) * WIDTH] = d_other[part]

    f[0:P_SIZE, P_SIZE:] = top[...]
    rows = lax.broadcasted_iota(jnp.int32, (P_SIZE, P_SIZE), 0)
    cols = lax.broadcasted_iota(jnp.int32, (P_SIZE, P_SIZE), 1)
    f[P_SIZE:, 0:P_SIZE] = jnp.where(rows == cols, 1.0, 0.0)
    f[P_SIZE:, P_SIZE:] = jnp.zeros((P_SIZE, WIDTH), jnp.float32)
    total = P_SIZE + WIDTH
    for block in range(P_SIZE // B):
        lo, hi = block * B, block * B + B
        base = lo // WIDTH * WIDTH
        r = lax.broadcasted_iota(jnp.int32, (WIDTH, WIDTH), 0) + base
        c = lax.broadcasted_iota(jnp.int32, (WIDTH, WIDTH), 1) + base
        in_block = (r >= lo) & (r < hi) & (c >= lo) & (c < hi)
        on_diag = in_block & (r == c)
        window = f[base : base + WIDTH, base : base + WIDTH]
        pivot = jnp.where(in_block, window, 0.0)
        diag = jnp.where(on_diag, window, 0.0)
        diag_row = jnp.sum(diag, axis=0, keepdims=True)
        diag_col = jnp.sum(diag, axis=1, keepdims=True)
        inv_row = 1.0 / jnp.where(diag_row == 0.0, 1.0, diag_row)
        inv_col = 1.0 / jnp.where(diag_col == 0.0, 1.0, diag_col)
        inverse = jnp.where(on_diag, 2.0 * inv_row, 0.0) - inv_col * (pivot * inv_row)
        for _ in range(ITERS - 1):
            inverse = 2.0 * inverse - stacked_dot(inverse, stacked_dot(pivot, inverse))
        lower = stacked_dot(f[hi:, base : base + WIDTH], inverse)
        left_col = hi // WIDTH * WIDTH
        col = lax.broadcasted_iota(jnp.int32, (WIDTH, total - left_col), 1) + left_col
        upper = jnp.where(col >= hi, f[base : base + WIDTH, left_col:], 0.0)
        f[hi:, left_col:] = f[hi:, left_col:] - stacked_dot(lower, upper)
        lane = lax.broadcasted_iota(jnp.int32, lower.shape, 1) + base
        mine = (lane >= lo) & (lane < hi)
        f[hi:, base : base + WIDTH] = jnp.where(mine, lower, f[hi:, base : base + WIDTH])

    def finish(update, done):
        high = update.astype(jnp.bfloat16)
        low = (update - high.astype(jnp.float32)).astype(jnp.bfloat16)
        update_out[...] = jnp.concatenate([high, low], axis=1)
        top_out[...] = done

    @pl.when(panel == 0)
    def _():
        finish(f[P_SIZE:, P_SIZE:], f[0:P_SIZE, P_SIZE:])

    for part in range(2):
        @pl.when((panel == 1) & (second == part))
        def _():
            side = slice(part * WIDTH, (part + 1) * WIDTH)
            finish(f[P_SIZE:, side], f[0:P_SIZE, side])


def factor(info, d_mine, d_other, top):
    vmem = pl.BlockSpec(memory_space=pltpu.VMEM)
    return pl.pallas_call(
        factor_kernel,
        out_shape=(pltpu.VMEM((P_SIZE, 2 * WIDTH), jnp.bfloat16), pltpu.VMEM((P_SIZE, WIDTH), jnp.float32)),
        in_specs=[pl.BlockSpec(memory_space=pltpu.SMEM), vmem, vmem, vmem],
        out_specs=(vmem, vmem),
        scratch_shapes=[pltpu.VMEM((2 * P_SIZE, P_SIZE + WIDTH), jnp.float32)],
        compiler_params=pltpu.CompilerParams(vmem_limit_bytes=4 << 20),
        cost_estimate=pl.CostEstimate(flops=9_000_000_000, bytes_accessed=2_000_000, transcendentals=0),
        name="factor",
    )(info, in_vmem(d_mine), in_vmem(d_other), in_vmem(top))


def update_body(places, info, front, parts, update, top, out):
    step = pl.program_id(0)

    for at in range(4):
        @pl.when(step == at)
        def _():
            panel = jnp.concatenate([parts[at][0], parts[at][1]], axis=1)
            high = panel.astype(jnp.bfloat16)
            low = (panel - high.astype(jnp.float32)).astype(jnp.bfloat16)
            both = jnp.dot(high, update[...], preferred_element_type=jnp.float32)
            both = both + jnp.dot(low, update[...], preferred_element_type=jnp.float32)
            out[...] = jnp.where(info[1] == 0, front[...], 0.0) + (both[:, :WIDTH] + both[:, WIDTH:])

    @pl.when((places[step] == 0) & (info[3] == 0))
    def _():
        out[0:P_SIZE, :] = top[...]


def first_update_kernel(places, info, front, p0, p1, p2, p3, update, top, out):
    update_body(places, info, front, (p0, p1, p2, p3), update, top, out)


def second_update_kernel(places, info, front, p0, p1, p2, p3, update, top, _, out):
    update_body(places, info, front, (p0, p1, p2, p3), update, top, out)


def apply_update(places, info, front, parts, update, top, done=None):
    vmem = pl.BlockSpec(memory_space=pltpu.VMEM)
    block = pl.BlockSpec((SHARE, WIDTH), lambda i, places, info: (places[i], 0))
    more = [] if done is None else [pl.BlockSpec(memory_space=pl.ANY)]
    extra = [] if done is None else [done]
    return pl.pallas_call(
        first_update_kernel if done is None else second_update_kernel,
        out_shape=jax.ShapeDtypeStruct((ROWS, WIDTH), jnp.float32),
        grid_spec=pltpu.PrefetchScalarGridSpec(
            num_scalar_prefetch=2,
            grid=(4,),
            in_specs=[block] + [vmem] * 6 + more,
            out_specs=block,
        ),
        input_output_aliases={} if done is None else {9: 0},
        compiler_params=pltpu.CompilerParams(vmem_limit_bytes=4 << 20),
        cost_estimate=pl.CostEstimate(flops=3_000_000_000, bytes_accessed=4_000_000, transcendentals=0),
        name="update_mine" if done is None else "update_other",
    )(places, info, pltpu.with_memory_space_constraint(front, pltpu.HBM), *map(in_vmem, parts), in_vmem(update), in_vmem(top), *extra)


def per_device(front):
    row, x, core, z, y = (lax.axis_index(a) for a in AXES)
    mine = coset(z, y)
    panel = (x == 0) & (z == 0) & (y < 2) & (core == 0)
    info = jnp.stack([core, panel.astype(jnp.int32), y, row]).astype(jnp.int32)

    d_part = jnp.where(core == 0, front[:DPART], send(front[DPART:P_SIZE], CORE_SWAP))
    beside = send(front, CORE_SWAP)

    def share(delta):
        start = (mine + delta) % 4 * SHARE
        kept = lax.dynamic_slice(front, (start, 0), (SHARE, WIDTH))
        given = lax.dynamic_slice(beside, (start + ROWS // 2, 0), (SHARE, WIDTH))
        return jnp.concatenate([d_part, jnp.where(core == 0, kept, given)])

    up = send(share(1), shift(1, 0))
    down = send(share(3), shift(-1, 0))
    side = send(share(2), SIDE)
    top_swapped = send(front[:P_SIZE], ROW_SWAP)
    top = jnp.where(row == 0, front[:P_SIZE], top_swapped)
    near = y < 2
    held = jnp.where((z == 1) & near, up, jnp.where((z == 3) & near, down, jnp.where(near, share(0), side)))
    held = jnp.where(x == 0, held, send(held, X_SWAP))

    to_first = send(held, FIRST_PAIRS)
    swapped = send(held, SWAP_PAIRS)
    to_second = send(held, SECOND_PAIRS)
    role = member(z, y)

    def pick(a, b, c, d):
        return jnp.where(role == 0, a, jnp.where(role == 1, b, jnp.where(role == 2, c, d)))

    left = pick(held, swapped, to_first, to_second)
    right = pick(swapped, held, to_second, to_first)
    d_mine = jnp.stack([left[:DPART], right[:DPART]])
    own = jnp.stack([left[DPART:], right[DPART:]])
    before = send(own, shift(1, 0))
    after = send(own, shift(-1, 0))
    far = send(own, shift(0, 1))
    d_mine = jnp.where(row == 0, d_mine, send(d_mine, ROW_SWAP))
    d_other = send(d_mine, CORE_SWAP)
    own_other = send(own, CORE_SWAP)
    update, top_done = factor(info, d_mine, d_other, top)

    parts = (own, before, after, far)
    others = (own_other, *(send(v, CORE_SWAP) for v in parts[1:]))
    order = [mine, (mine + 3) % 4, (mine + 1) % 4, (mine + 2) % 4]
    places = [jnp.stack([p + 4 * c for p in order]).astype(jnp.int32) for c in (core, 1 - core)]
    out = apply_update(places[0], info, front, parts, update, top_done)
    return apply_update(places[1], info, front, others, update, top_done, out)


def solution(mesh):
    wide = jax.sharding.Mesh(mesh.devices.reshape(SHAPE), AXES)
    spec = P("row", ("x", "core", "z", "y"))

    return jax.shard_map(per_device, mesh=wide, in_specs=(spec,), out_specs=spec, check_vma=False)
```

```python
import jax
import jax.numpy as jnp
from jax import lax
from jax.experimental import pallas as pl
from jax.experimental.pallas import tpu as pltpu
from jax.sharding import PartitionSpec as P


B = 64
ITERS = 2
P_SIZE = 256

AXES = ("row", "x", "core", "z", "y")
SHAPE = (2, 2, 2, 4, 4)
ROWS = 4096
WIDTH = 128
SHARE = 512
DPART = 128


def place(r, x, c, z, y):
    return (((r * 2 + x) * 2 + c) * 4 + z % 4) * 4 + y % 4


def everywhere(zy_pairs, xs=(0, 1)):
    return [
        (place(r, x, c, *a), place(r, x, c, *b)) for r in range(2) for x in xs for c in range(2) for a, b in zy_pairs
    ]


ALL_ZY = [(z, y) for z in range(4) for y in range(4)]


def shift(dz, dy):
    return everywhere([((z, y), (z + dz, y + dy)) for z, y in ALL_ZY])


ROW_DOWN = [(place(0, x, c, z, y), place(1, x, c, z, y)) for x in range(2) for c in range(2) for z, y in ALL_ZY]
CORE_SWAP = [
    (place(r, x, c, z, y), place(r, x, 1 - c, z, y)) for r in range(2) for x in range(2) for c in range(2) for z, y in ALL_ZY
]
X_SWAP = [
    (place(r, x, c, z, y), place(r, 1 - x, c, z, y)) for r in range(2) for x in range(2) for c in range(2) for z, y in ALL_ZY
]


def coset(z, y):
    return (z + 2 * y) % 4


SIDE = everywhere([((z, y), (z, 3 - y)) for z, y in ALL_ZY])
ROW_SWAP = ROW_DOWN + [(b, a) for a, b in ROW_DOWN]


def member(z, y):
    near = ((y == 0) & (z != 2)) | ((y == 3) & (z == 0))
    far = ((y == 1) & (z != 2)) | ((y == 2) & (z == 0))
    third = ((y == 2) & (z != 0)) | ((y == 1) & (z == 2))
    return 3 - 3 * near - 2 * far - third


def member_pairs():
    spread, trade = [], []
    for c in range(4):
        m = {int(member(z, y)): (z, y) for z, y in ALL_ZY if coset(z, y) == c}
        spread += [(m[0], m[2]), (m[1], m[3])]
        trade += [(m[0], m[1]), (m[1], m[0]), (m[2], m[3]), (m[3], m[2])]
    return everywhere(spread), everywhere(trade)


SPREAD, TRADE = member_pairs()


def send(value, pairs):
    return lax.ppermute(value, AXES, pairs)


def in_vmem(value):
    return pltpu.with_memory_space_constraint(value, pltpu.VMEM)


def split3(value):
    high = value.astype(jnp.bfloat16)
    rest = value - high.astype(jnp.float32)
    middle = rest.astype(jnp.bfloat16)
    low = (rest - middle.astype(jnp.float32)).astype(jnp.bfloat16)
    return high, middle, low


def stacked_dot(left, right):
    lh, lm, ll = split3(left)
    rh, rm, rl = split3(right)
    lefts = jnp.concatenate([ll, lh, lm, lm, lh, lh], axis=1)
    rights = jnp.concatenate([rh, rl, rm, rh, rm, rh], axis=0)
    return jnp.dot(lefts, rights, preferred_element_type=jnp.float32)


def factor_kernel(info, d_mine, d_other, top, update_out, top_out, f):
    core, panel, second = info[0], info[1], info[2]
    for half in range(2):
        @pl.when(core == half)
        def _():
            for part in range(2):
                f[half * DPART : (half + 1) * DPART, part * WIDTH : (part + 1) * WIDTH] = d_mine[part]
                f[(1 - half) * DPART : (2 - half) * DPART, part * WIDTH : (part + 1) * WIDTH] = d_other[part]

    f[0:P_SIZE, P_SIZE:] = top[...]
    rows = lax.broadcasted_iota(jnp.int32, (P_SIZE, P_SIZE), 0)
    cols = lax.broadcasted_iota(jnp.int32, (P_SIZE, P_SIZE), 1)
    f[P_SIZE:, 0:P_SIZE] = jnp.where(rows == cols, 1.0, 0.0)
    f[P_SIZE:, P_SIZE:] = jnp.zeros((P_SIZE, WIDTH), jnp.float32)
    total = P_SIZE + WIDTH
    for block in range(P_SIZE // B):
        lo, hi = block * B, block * B + B
        base = lo // WIDTH * WIDTH
        r = lax.broadcasted_iota(jnp.int32, (WIDTH, WIDTH), 0) + base
        c = lax.broadcasted_iota(jnp.int32, (WIDTH, WIDTH), 1) + base
        in_block = (r >= lo) & (r < hi) & (c >= lo) & (c < hi)
        on_diag = in_block & (r == c)
        window = f[base : base + WIDTH, base : base + WIDTH]
        pivot = jnp.where(in_block, window, 0.0)
        diag = jnp.where(on_diag, window, 0.0)
        diag_row = jnp.sum(diag, axis=0, keepdims=True)
        diag_col = jnp.sum(diag, axis=1, keepdims=True)
        inv_row = 1.0 / jnp.where(diag_row == 0.0, 1.0, diag_row)
        inv_col = 1.0 / jnp.where(diag_col == 0.0, 1.0, diag_col)
        inverse = jnp.where(on_diag, 2.0 * inv_row, 0.0) - inv_col * (pivot * inv_row)
        for _ in range(ITERS - 1):
            inverse = 2.0 * inverse - stacked_dot(inverse, stacked_dot(pivot, inverse))
        lower = stacked_dot(f[hi:, base : base + WIDTH], inverse)
        left_col = hi // WIDTH * WIDTH
        col = lax.broadcasted_iota(jnp.int32, (WIDTH, total - left_col), 1) + left_col
        upper = jnp.where(col >= hi, f[base : base + WIDTH, left_col:], 0.0)
        f[hi:, left_col:] = f[hi:, left_col:] - stacked_dot(lower, upper)
        lane = lax.broadcasted_iota(jnp.int32, lower.shape, 1) + base
        mine = (lane >= lo) & (lane < hi)
        f[hi:, base : base + WIDTH] = jnp.where(mine, lower, f[hi:, base : base + WIDTH])

    def finish(update, done):
        high = update.astype(jnp.bfloat16)
        low = (update - high.astype(jnp.float32)).astype(jnp.bfloat16)
        update_out[...] = jnp.concatenate([high, low], axis=1)
        top_out[...] = done

    @pl.when(panel == 0)
    def _():
        finish(f[P_SIZE:, P_SIZE:], f[0:P_SIZE, P_SIZE:])

    for part in range(2):
        @pl.when((panel == 1) & (second == part))
        def _():
            side = slice(part * WIDTH, (part + 1) * WIDTH)
            finish(f[P_SIZE:, side], f[0:P_SIZE, side])


def factor(info, d_mine, d_other, top):
    vmem = pl.BlockSpec(memory_space=pltpu.VMEM)
    return pl.pallas_call(
        factor_kernel,
        out_shape=(pltpu.VMEM((P_SIZE, 2 * WIDTH), jnp.bfloat16), pltpu.VMEM((P_SIZE, WIDTH), jnp.float32)),
        in_specs=[pl.BlockSpec(memory_space=pltpu.SMEM), vmem, vmem, vmem],
        out_specs=(vmem, vmem),
        scratch_shapes=[pltpu.VMEM((2 * P_SIZE, P_SIZE + WIDTH), jnp.float32)],
        compiler_params=pltpu.CompilerParams(vmem_limit_bytes=4 << 20),
        cost_estimate=pl.CostEstimate(flops=9_000_000_000, bytes_accessed=2_000_000, transcendentals=0),
        name="factor",
    )(info, in_vmem(d_mine), in_vmem(d_other), in_vmem(top))


def update_body(steps, places, info, front, parts, update, top, out):
    step = pl.program_id(0)
    for at in range(steps):
        @pl.when(step == at)
        def _():
            panel = jnp.concatenate([parts[at][0], parts[at][1]], axis=1)
            high = panel.astype(jnp.bfloat16)
            low = (panel - high.astype(jnp.float32)).astype(jnp.bfloat16)
            both = jnp.dot(high, update[...], preferred_element_type=jnp.float32)
            both = both + jnp.dot(low, update[...], preferred_element_type=jnp.float32)
            out[...] = jnp.where(info[1] == 0, front[...], 0.0) + (both[:, :WIDTH] + both[:, WIDTH:])

    @pl.when((places[step] == 0) & (info[3] == 0))
    def _():
        out[0:P_SIZE, :] = top[...]


def first_update_kernel(places, info, front, p0, p1, update, top, out):
    update_body(2, places, info, front, (p0, p1), update, top, out)


def later_update_kernel(places, info, front, p0, p1, p2, update, top, _, out):
    update_body(3, places, info, front, (p0, p1, p2), update, top, out)


def apply_update(places, info, front, parts, update, top, done=None):
    vmem = pl.BlockSpec(memory_space=pltpu.VMEM)
    block = pl.BlockSpec((SHARE, WIDTH), lambda i, places, info: (places[i], 0))
    more = [] if done is None else [pl.BlockSpec(memory_space=pl.ANY)]
    extra = [] if done is None else [done]
    front = pltpu.with_memory_space_constraint(front, pltpu.HBM)
    return pl.pallas_call(
        first_update_kernel if done is None else later_update_kernel,
        out_shape=jax.ShapeDtypeStruct((ROWS, WIDTH), jnp.float32),
        grid_spec=pltpu.PrefetchScalarGridSpec(
            num_scalar_prefetch=2,
            grid=(len(parts),),
            in_specs=[block] + [vmem] * (len(parts) + 2) + more,
            out_specs=block,
        ),
        input_output_aliases={} if done is None else {8: 0},
        compiler_params=pltpu.CompilerParams(vmem_limit_bytes=4 << 20),
        cost_estimate=pl.CostEstimate(flops=3_000_000_000, bytes_accessed=4_000_000, transcendentals=0),
    )(places, info, front, *map(in_vmem, parts), in_vmem(update), in_vmem(top), *extra)


def per_device(front):
    row, x, core, z, y = (lax.axis_index(a) for a in AXES)
    mine = coset(z, y)
    panel = (x == 0) & (z == 0) & (y < 2) & (core == 0)
    info = jnp.stack([core, panel.astype(jnp.int32), y, row]).astype(jnp.int32)

    def start(delta):
        return (mine + delta) % 4 * SHARE

    def rows(array, at, size=SHARE):
        return lax.dynamic_slice(array, (at, 0), (size, WIDTH))

    early = lax.optimization_barrier(front)
    kept = jnp.concatenate([early[:DPART], rows(early, start(1))])
    given = jnp.concatenate([early[DPART:P_SIZE], rows(early, start(1) + ROWS // 2)])
    to_up = jnp.where(core == 0, kept, send(given, CORE_SWAP))
    beside = send(front, CORE_SWAP)
    up = send(to_up, shift(1, 0))

    def share(delta):
        half = jnp.where(core == 0, rows(front, start(delta)), rows(beside, start(delta) + ROWS // 2))
        return jnp.concatenate([to_up[:DPART], half])

    down = send(share(3), shift(-1, 0))
    side = send(share(2), SIDE)
    near = y < 2
    held = jnp.where((z == 1) & near, up, jnp.where((z == 3) & near, down, jnp.where(near, share(0), side)))
    held = jnp.where(x == 0, held, send(held, X_SWAP))

    role = member(z, y)
    part = jnp.where(role < 2, held, send(held, SPREAD))
    top_swapped = send(front[:P_SIZE], ROW_SWAP)
    top = jnp.where(row == 0, front[:P_SIZE], top_swapped)
    part, d_part = part[DPART:], part[:DPART]
    other = send(part, TRADE)
    d_part = jnp.where(row == 0, d_part, send(d_part, ROW_SWAP))
    d_traded = send(d_part, TRADE)

    def in_order(a, b):
        first = role % 2 == 0
        return jnp.stack([jnp.where(first, a, b), jnp.where(first, b, a)])

    own = in_order(part, other)
    d_mine = in_order(d_part, d_traded)
    before = send(own, shift(1, 0))
    after = send(own, shift(-1, 0))
    far = send(own, shift(0, 1))
    d_other = send(d_mine, CORE_SWAP)
    own_other = send(own, CORE_SWAP)
    update, top_done = factor(info, d_mine, d_other, top)

    order = [(mine + 3) % 4, (mine + 1) % 4, (mine + 2) % 4]

    def at(*blocks):
        return jnp.stack(blocks).astype(jnp.int32)

    out = apply_update(at(mine + 4 * core, mine + 4 * (1 - core)), info, front, (own, own_other), update, top_done)
    received = (before, after, far)
    others = tuple(send(v, CORE_SWAP) for v in received)
    places = at(*(p + 4 * core for p in order))
    out = apply_update(places, info, front, received, update, top_done, out)
    places = at(*(p + 4 * (1 - core) for p in order))
    return apply_update(places, info, front, others, update, top_done, out)


def solution(mesh):
    wide = jax.sharding.Mesh(mesh.devices.reshape(SHAPE), AXES)
    spec = P("row", ("x", "core", "z", "y"))

    return jax.shard_map(per_device, mesh=wide, in_specs=(spec,), out_specs=spec, check_vma=False)
```

```python
import jax
import jax.numpy as jnp
from jax import lax
from jax.experimental import pallas as pl
from jax.experimental.pallas import tpu as pltpu
from jax.sharding import PartitionSpec as P


B = 64
ITERS = 2
P_SIZE = 256

AXES = ("row", "x", "core", "z", "y")
SHAPE = (2, 2, 2, 4, 4)
ROWS = 4096
WIDTH = 128
SHARE = 512
DPART = 128


def place(r, x, c, z, y):
    return (((r * 2 + x) * 2 + c) * 4 + z % 4) * 4 + y % 4


def everywhere(zy_pairs, xs=(0, 1)):
    return [
        (place(r, x, c, *a), place(r, x, c, *b)) for r in range(2) for x in xs for c in range(2) for a, b in zy_pairs
    ]


ALL_ZY = [(z, y) for z in range(4) for y in range(4)]


def shift(dz, dy):
    return everywhere([((z, y), (z + dz, y + dy)) for z, y in ALL_ZY])


ROW_DOWN = [(place(0, x, c, z, y), place(1, x, c, z, y)) for x in range(2) for c in range(2) for z, y in ALL_ZY]
CORE_SWAP = [
    (place(r, x, c, z, y), place(r, x, 1 - c, z, y)) for r in range(2) for x in range(2) for c in range(2) for z, y in ALL_ZY
]
X_SWAP = [
    (place(r, x, c, z, y), place(r, 1 - x, c, z, y)) for r in range(2) for x in range(2) for c in range(2) for z, y in ALL_ZY
]


def coset(z, y):
    return (z + 2 * y) % 4


UP = everywhere([((0, 0), (1, 0)), ((0, 1), (1, 1))], xs=(0,))
DOWN = everywhere([((0, 0), (3, 0)), ((0, 1), (3, 1))], xs=(0,))
SIDE = everywhere([((0, 0), (0, 3)), ((0, 1), (0, 2))], xs=(0,))
ROW_SWAP = ROW_DOWN + [(b, a) for a, b in ROW_DOWN]


def member(z, y):
    near = ((y == 0) & (z != 2)) | ((y == 3) & (z == 0))
    far = ((y == 1) & (z != 2)) | ((y == 2) & (z == 0))
    third = ((y == 2) & (z != 0)) | ((y == 1) & (z == 2))
    return 3 - 3 * near - 2 * far - third


def member_pairs():
    spread, trade = [], []
    for c in range(4):
        m = {int(member(z, y)): (z, y) for z, y in ALL_ZY if coset(z, y) == c}
        spread += [(m[0], m[2]), (m[1], m[3])]
        trade += [(m[0], m[1]), (m[1], m[0]), (m[2], m[3]), (m[3], m[2])]
    return everywhere(spread), everywhere(trade)


SPREAD, TRADE = member_pairs()


def send(value, pairs):
    return lax.ppermute(value, AXES, pairs)


def in_vmem(value):
    return pltpu.with_memory_space_constraint(value, pltpu.VMEM)


def split3(value):
    high = value.astype(jnp.bfloat16)
    rest = value - high.astype(jnp.float32)
    middle = rest.astype(jnp.bfloat16)
    low = (rest - middle.astype(jnp.float32)).astype(jnp.bfloat16)
    return high, middle, low


def stacked_dot(left, right):
    lh, lm, ll = split3(left)
    rh, rm, rl = split3(right)
    lefts = jnp.concatenate([ll, lh, lm, lm, lh, lh], axis=1)
    rights = jnp.concatenate([rh, rl, rm, rh, rm, rh], axis=0)
    return jnp.dot(lefts, rights, preferred_element_type=jnp.float32)


def factor_kernel(info, d_mine, d_other, top, update_out, top_out, f, sem):
    core = info[0]
    kind = jnp.where(info[1] == 0, 0, info[2] + 1)
    sides = (slice(P_SIZE, P_SIZE + WIDTH), slice(0, WIDTH), slice(WIDTH, P_SIZE))
    for half in range(2):
        @pl.when(core == half)
        def _():
            for part in range(2):
                f[half * DPART : (half + 1) * DPART, part * WIDTH : (part + 1) * WIDTH] = d_mine[part]
                f[(1 - half) * DPART : (2 - half) * DPART, part * WIDTH : (part + 1) * WIDTH] = d_other[part]

    f[0:P_SIZE, P_SIZE:] = top[...]
    rows = lax.broadcasted_iota(jnp.int32, (P_SIZE, P_SIZE), 0)
    cols = lax.broadcasted_iota(jnp.int32, (P_SIZE, P_SIZE), 1)
    f[P_SIZE:, 0:P_SIZE] = jnp.where(rows == cols, 1.0, 0.0)
    f[P_SIZE:, P_SIZE:] = jnp.zeros((P_SIZE, WIDTH), jnp.float32)
    total = P_SIZE + WIDTH
    for block in range(P_SIZE // B):
        lo, hi = block * B, block * B + B
        base = lo // WIDTH * WIDTH
        r = lax.broadcasted_iota(jnp.int32, (WIDTH, WIDTH), 0) + base
        c = lax.broadcasted_iota(jnp.int32, (WIDTH, WIDTH), 1) + base
        in_block = (r >= lo) & (r < hi) & (c >= lo) & (c < hi)
        on_diag = in_block & (r == c)
        window = f[base : base + WIDTH, base : base + WIDTH]
        pivot = jnp.where(in_block, window, 0.0)
        diag = jnp.where(on_diag, window, 0.0)
        diag_row = jnp.sum(diag, axis=0, keepdims=True)
        diag_col = jnp.sum(diag, axis=1, keepdims=True)
        inv_row = 1.0 / jnp.where(diag_row == 0.0, 1.0, diag_row)
        inv_col = 1.0 / jnp.where(diag_col == 0.0, 1.0, diag_col)
        inverse = jnp.where(on_diag, 2.0 * inv_row, 0.0) - inv_col * (pivot * inv_row)
        for _ in range(ITERS - 1):
            inverse = 2.0 * inverse - stacked_dot(inverse, stacked_dot(pivot, inverse))
        lower = stacked_dot(f[hi:, base : base + WIDTH], inverse)
        left_col = hi // WIDTH * WIDTH
        col = lax.broadcasted_iota(jnp.int32, (WIDTH, total - left_col), 1) + left_col
        upper = jnp.where(col >= hi, f[base : base + WIDTH, left_col:], 0.0)
        f[hi:, left_col:] = f[hi:, left_col:] - stacked_dot(lower, upper)
        lane = lax.broadcasted_iota(jnp.int32, lower.shape, 1) + base
        mine = (lane >= lo) & (lane < hi)
        f[hi:, base : base + WIDTH] = jnp.where(mine, lower, f[hi:, base : base + WIDTH])
        if block == P_SIZE // B - 2:
            for case, side in enumerate(sides):
                @pl.when(kind == case)
                def _():
                    pltpu.make_async_copy(f.at[0:P_SIZE, side], top_out, sem).start()

    def finish(update):
        high = update.astype(jnp.bfloat16)
        low = (update - high.astype(jnp.float32)).astype(jnp.bfloat16)
        update_out[...] = jnp.concatenate([high, low], axis=1)

    for case, side in enumerate(sides):
        @pl.when(kind == case)
        def _():
            finish(f[P_SIZE:, side])

    pltpu.make_async_copy(f.at[0:P_SIZE, sides[0]], top_out, sem).wait()


def factor(info, d_mine, d_other, top):
    vmem = pl.BlockSpec(memory_space=pltpu.VMEM)
    return pl.pallas_call(
        factor_kernel,
        out_shape=(pltpu.VMEM((P_SIZE, 2 * WIDTH), jnp.bfloat16), pltpu.HBM((P_SIZE, WIDTH), jnp.float32)),
        in_specs=[pl.BlockSpec(memory_space=pltpu.SMEM), vmem, vmem, vmem],
        out_specs=(vmem, pl.BlockSpec(memory_space=pltpu.HBM)),
        scratch_shapes=[pltpu.VMEM((2 * P_SIZE, P_SIZE + WIDTH), jnp.float32), pltpu.SemaphoreType.DMA],
        compiler_params=pltpu.CompilerParams(vmem_limit_bytes=4 << 20),
        cost_estimate=pl.CostEstimate(flops=9_000_000_000, bytes_accessed=2_000_000, transcendentals=0),
        name="factor",
    )(info, in_vmem(d_mine), in_vmem(d_other), in_vmem(top))


def update_kernel(info, front, *refs):
    out, blocks, top_rows, loads, stores, top_sem = refs[-6:]
    count = blocks.shape[0]
    parts, update, top = refs[:count], refs[count], refs[count + 1]
    top_load = pltpu.make_async_copy(top, top_rows, top_sem)
    has_top = [(info[2 + at] == 0) & (info[1] == 0) for at in range(count)]

    def load(at):
        rows = pl.ds(pl.multiple_of(info[2 + at] * SHARE, SHARE), SHARE)
        return pltpu.make_async_copy(front.at[rows, :], blocks.at[at], loads.at[at])

    def store(at):
        rows = pl.ds(pl.multiple_of(info[2 + at] * SHARE, SHARE), SHARE)
        return pltpu.make_async_copy(blocks.at[at], out.at[rows, :], stores.at[at])

    for at in range(count):
        load(at).start()
        pl.when(has_top[at])(top_load.start)
    for at in range(count):
        panel = jnp.concatenate([parts[at][0], parts[at][1]], axis=1)
        high = panel.astype(jnp.bfloat16)
        low = (panel - high.astype(jnp.float32)).astype(jnp.bfloat16)
        both = jnp.dot(high, update[...], preferred_element_type=jnp.float32)
        both = both + jnp.dot(low, update[...], preferred_element_type=jnp.float32)
        added = both[:, :WIDTH] + both[:, WIDTH:]
        load(at).wait()
        blocks[at] = jnp.where(info[0] == 0, blocks[at], 0.0) + added

        @pl.when(has_top[at])
        def _():
            top_load.wait()
            blocks[at, 0:P_SIZE, :] = top_rows[...]

        store(at).start()
    for at in range(count):
        store(at).wait()


def apply_update(info, front, parts, update, top, done=None):
    vmem, hbm = pl.BlockSpec(memory_space=pltpu.VMEM), pl.BlockSpec(memory_space=pltpu.HBM)
    count = len(parts)
    front = pltpu.with_memory_space_constraint(front, pltpu.HBM)
    return pl.pallas_call(
        update_kernel,
        out_shape=jax.ShapeDtypeStruct((ROWS, WIDTH), jnp.float32),
        in_specs=[pl.BlockSpec(memory_space=pltpu.SMEM), hbm] + [vmem] * (count + 1) + [hbm] * (1 + (done is not None)),
        out_specs=hbm,
        scratch_shapes=[
            pltpu.VMEM((count, SHARE, WIDTH), jnp.float32),
            pltpu.VMEM((P_SIZE, WIDTH), jnp.float32),
            pltpu.SemaphoreType.DMA((count,)),
            pltpu.SemaphoreType.DMA((count,)),
            pltpu.SemaphoreType.DMA,
        ],
        input_output_aliases={} if done is None else {count + 4: 0},
        compiler_params=pltpu.CompilerParams(vmem_limit_bytes=4 << 20),
        cost_estimate=pl.CostEstimate(flops=3_000_000_000, bytes_accessed=4_000_000, transcendentals=0),
    )(info, front, *map(in_vmem, parts), in_vmem(update), pltpu.with_memory_space_constraint(top, pltpu.HBM), *([] if done is None else [done]))


def per_device(front):
    row, x, core, z, y = (lax.axis_index(a) for a in AXES)
    mine = coset(z, y)
    panel = (x == 0) & (z == 0) & (y < 2) & (core == 0)
    info = jnp.stack([core, panel.astype(jnp.int32), y, row]).astype(jnp.int32)

    def start(delta):
        return (mine + delta) % 4 * SHARE

    def rows(array, at, size=SHARE):
        return lax.dynamic_slice(array, (at, 0), (size, WIDTH))

    early = lax.optimization_barrier(front)
    kept = jnp.concatenate([early[:DPART], rows(early, start(1))])
    given = jnp.concatenate([early[DPART:P_SIZE], rows(early, start(1) + ROWS // 2)])
    to_up = jnp.where(core == 0, kept, send(given, CORE_SWAP))
    beside = send(front, CORE_SWAP)
    up = send(to_up, UP)

    def share(delta):
        half = jnp.where(core == 0, rows(front, start(delta)), rows(beside, start(delta) + ROWS // 2))
        return jnp.concatenate([to_up[:DPART], half])

    down = send(share(3), DOWN)
    side = send(share(2), SIDE)
    near = y < 2
    held = jnp.where((z == 1) & near, up, jnp.where((z == 3) & near, down, jnp.where(near, share(0), side)))
    held = jnp.where(x == 0, held, send(held, X_SWAP))

    role = member(z, y)
    part = jnp.where(role < 2, held, send(held, SPREAD))
    top_swapped = send(front[:P_SIZE], ROW_SWAP)
    top = jnp.where(row == 0, front[:P_SIZE], top_swapped)
    part, d_part = part[DPART:], part[:DPART]
    other = send(part, TRADE)
    d_part = jnp.where(row == 0, d_part, send(d_part, ROW_SWAP))
    d_traded = send(d_part, TRADE)

    def in_order(a, b):
        first = role % 2 == 0
        return jnp.stack([jnp.where(first, a, b), jnp.where(first, b, a)])

    own = in_order(part, other)
    d_mine = in_order(d_part, d_traded)
    before = send(own, shift(1, 0))
    after = send(own, shift(-1, 0))
    far = send(own, shift(0, 1))
    d_other = send(d_mine, CORE_SWAP)
    own_other = send(own, CORE_SWAP)
    update, top_done = factor(info, d_mine, d_other, top)

    order = [(mine + 3) % 4, (mine + 1) % 4, (mine + 2) % 4]

    def at(*blocks):
        return jnp.stack([panel.astype(jnp.int32), row, *blocks]).astype(jnp.int32)

    places = at(mine + 4 * core, mine + 4 * (1 - core))
    out = apply_update(places, front, (own, own_other), update, top_done)
    received = (before, after, far)
    others = tuple(send(v, CORE_SWAP) for v in received)
    places = at(*(p + 4 * core for p in order))
    out = apply_update(places, front, received, update, top_done, out)
    places = at(*(p + 4 * (1 - core) for p in order))
    return apply_update(places, front, others, update, top_done, out)


def solution(mesh):
    wide = jax.sharding.Mesh(mesh.devices.reshape(SHAPE), AXES)
    spec = P("row", ("x", "core", "z", "y"))

    return jax.shard_map(per_device, mesh=wide, in_specs=(spec,), out_specs=spec, check_vma=False)
```

```python
import jax
import jax.numpy as jnp
from jax import lax
from jax.experimental import pallas as pl
from jax.experimental.pallas import tpu as pltpu
from jax.sharding import PartitionSpec as P


B = 64
ITERS = 2
P_SIZE = 256

AXES = ("row", "x", "core", "z", "y")
SHAPE = (2, 2, 2, 4, 4)
ROWS = 4096
WIDTH = 128
SHARE = 512
DPART = 128


def place(r, x, c, z, y):
    return (((r * 2 + x) * 2 + c) * 4 + z % 4) * 4 + y % 4


def everywhere(zy_pairs, xs=(0, 1)):
    return [
        (place(r, x, c, *a), place(r, x, c, *b)) for r in range(2) for x in xs for c in range(2) for a, b in zy_pairs
    ]


ALL_ZY = [(z, y) for z in range(4) for y in range(4)]


def shift(dz, dy):
    return everywhere([((z, y), (z + dz, y + dy)) for z, y in ALL_ZY])


ROW_DOWN = [(place(0, x, c, z, y), place(1, x, c, z, y)) for x in range(2) for c in range(2) for z, y in ALL_ZY]
CORE_SWAP = [
    (place(r, x, c, z, y), place(r, x, 1 - c, z, y)) for r in range(2) for x in range(2) for c in range(2) for z, y in ALL_ZY
]
X_SWAP = [
    (place(r, x, c, z, y), place(r, 1 - x, c, z, y)) for r in range(2) for x in range(2) for c in range(2) for z, y in ALL_ZY
]


def coset(z, y):
    return (z + 2 * y) % 4


SIDE = everywhere([((z, y), (z, 3 - y)) for z, y in ALL_ZY])
ROW_SWAP = ROW_DOWN + [(b, a) for a, b in ROW_DOWN]


def member(z, y):
    near = ((y == 0) & (z != 2)) | ((y == 3) & (z == 0))
    far = ((y == 1) & (z != 2)) | ((y == 2) & (z == 0))
    third = ((y == 2) & (z != 0)) | ((y == 1) & (z == 2))
    return 3 - 3 * near - 2 * far - third


def member_pairs():
    spread, trade = [], []
    for c in range(4):
        m = {int(member(z, y)): (z, y) for z, y in ALL_ZY if coset(z, y) == c}
        spread += [(m[0], m[2]), (m[1], m[3])]
        trade += [(m[0], m[1]), (m[1], m[0]), (m[2], m[3]), (m[3], m[2])]
    return everywhere(spread), everywhere(trade)


SPREAD, TRADE = member_pairs()


def send(value, pairs):
    return lax.ppermute(value, AXES, pairs)


def in_vmem(value):
    return pltpu.with_memory_space_constraint(value, pltpu.VMEM)


def split3(value):
    high = value.astype(jnp.bfloat16)
    rest = value - high.astype(jnp.float32)
    middle = rest.astype(jnp.bfloat16)
    low = (rest - middle.astype(jnp.float32)).astype(jnp.bfloat16)
    return high, middle, low


def stacked_dot(left, right):
    lh, lm, ll = split3(left)
    rh, rm, rl = split3(right)
    lefts = jnp.concatenate([ll, lh, lm, lm, lh, lh], axis=1)
    rights = jnp.concatenate([rh, rl, rm, rh, rm, rh], axis=0)
    return jnp.dot(lefts, rights, preferred_element_type=jnp.float32)


def factor_kernel(info, d_mine, d_other, top, update_out, top_out, f, sem):
    core = info[0]
    kind = jnp.where(info[1] == 0, 0, info[2] + 1)
    sides = (slice(P_SIZE, P_SIZE + WIDTH), slice(0, WIDTH), slice(WIDTH, P_SIZE))
    for half in range(2):
        @pl.when(core == half)
        def _():
            for part in range(2):
                f[half * DPART : (half + 1) * DPART, part * WIDTH : (part + 1) * WIDTH] = d_mine[part]
                f[(1 - half) * DPART : (2 - half) * DPART, part * WIDTH : (part + 1) * WIDTH] = d_other[part]

    f[0:P_SIZE, P_SIZE:] = top[...]
    rows = lax.broadcasted_iota(jnp.int32, (P_SIZE, P_SIZE), 0)
    cols = lax.broadcasted_iota(jnp.int32, (P_SIZE, P_SIZE), 1)
    f[P_SIZE:, 0:P_SIZE] = jnp.where(rows == cols, 1.0, 0.0)
    f[P_SIZE:, P_SIZE:] = jnp.zeros((P_SIZE, WIDTH), jnp.float32)
    total = P_SIZE + WIDTH
    for block in range(P_SIZE // B):
        lo, hi = block * B, block * B + B
        base = lo // WIDTH * WIDTH
        r = lax.broadcasted_iota(jnp.int32, (WIDTH, WIDTH), 0) + base
        c = lax.broadcasted_iota(jnp.int32, (WIDTH, WIDTH), 1) + base
        in_block = (r >= lo) & (r < hi) & (c >= lo) & (c < hi)
        on_diag = in_block & (r == c)
        window = f[base : base + WIDTH, base : base + WIDTH]
        pivot = jnp.where(in_block, window, 0.0)
        diag = jnp.where(on_diag, window, 0.0)
        diag_row = jnp.sum(diag, axis=0, keepdims=True)
        diag_col = jnp.sum(diag, axis=1, keepdims=True)
        inv_row = 1.0 / jnp.where(diag_row == 0.0, 1.0, diag_row)
        inv_col = 1.0 / jnp.where(diag_col == 0.0, 1.0, diag_col)
        inverse = jnp.where(on_diag, 2.0 * inv_row, 0.0) - inv_col * (pivot * inv_row)
        for _ in range(ITERS - 1):
            inverse = 2.0 * inverse - stacked_dot(inverse, stacked_dot(pivot, inverse))
        lower = stacked_dot(f[hi:, base : base + WIDTH], inverse)
        left_col = hi // WIDTH * WIDTH
        col = lax.broadcasted_iota(jnp.int32, (WIDTH, total - left_col), 1) + left_col
        upper = jnp.where(col >= hi, f[base : base + WIDTH, left_col:], 0.0)
        f[hi:, left_col:] = f[hi:, left_col:] - stacked_dot(lower, upper)
        lane = lax.broadcasted_iota(jnp.int32, lower.shape, 1) + base
        mine = (lane >= lo) & (lane < hi)
        f[hi:, base : base + WIDTH] = jnp.where(mine, lower, f[hi:, base : base + WIDTH])
        if block == P_SIZE // B - 2:
            for case, side in enumerate(sides):
                @pl.when(kind == case)
                def _():
                    pltpu.make_async_copy(f.at[0:P_SIZE, side], top_out, sem).start()

    def finish(update):
        high = update.astype(jnp.bfloat16)
        low = (update - high.astype(jnp.float32)).astype(jnp.bfloat16)
        update_out[...] = jnp.concatenate([high, low], axis=1)

    for case, side in enumerate(sides):
        @pl.when(kind == case)
        def _():
            finish(f[P_SIZE:, side])

    pltpu.make_async_copy(f.at[0:P_SIZE, sides[0]], top_out, sem).wait()


def factor(info, d_mine, d_other, top):
    vmem = pl.BlockSpec(memory_space=pltpu.VMEM)
    return pl.pallas_call(
        factor_kernel,
        out_shape=(pltpu.VMEM((P_SIZE, 2 * WIDTH), jnp.bfloat16), pltpu.HBM((P_SIZE, WIDTH), jnp.float32)),
        in_specs=[pl.BlockSpec(memory_space=pltpu.SMEM), vmem, vmem, vmem],
        out_specs=(vmem, pl.BlockSpec(memory_space=pltpu.HBM)),
        scratch_shapes=[pltpu.VMEM((2 * P_SIZE, P_SIZE + WIDTH), jnp.float32), pltpu.SemaphoreType.DMA],
        compiler_params=pltpu.CompilerParams(vmem_limit_bytes=4 << 20),
        cost_estimate=pl.CostEstimate(flops=9_000_000_000, bytes_accessed=2_000_000, transcendentals=0),
        name="factor",
    )(info, in_vmem(d_mine), in_vmem(d_other), in_vmem(top))


def update_kernel(info, front, *refs):
    out, blocks, top_rows, loads, stores, top_sem = refs[-6:]
    count = blocks.shape[0]
    parts, update, top = refs[:count], refs[count], refs[count + 1]
    top_load = pltpu.make_async_copy(top, top_rows, top_sem)
    has_top = [(info[2 + at] == 0) & (info[1] == 0) for at in range(count)]

    def load(at):
        rows = pl.ds(pl.multiple_of(info[2 + at] * SHARE, SHARE), SHARE)
        return pltpu.make_async_copy(front.at[rows, :], blocks.at[at], loads.at[at])

    def store(at):
        rows = pl.ds(pl.multiple_of(info[2 + at] * SHARE, SHARE), SHARE)
        return pltpu.make_async_copy(blocks.at[at], out.at[rows, :], stores.at[at])

    for at in range(count):
        load(at).start()
        pl.when(has_top[at])(top_load.start)
    for at in range(count):
        panel = jnp.concatenate([parts[at][0], parts[at][1]], axis=1)
        high = panel.astype(jnp.bfloat16)
        low = (panel - high.astype(jnp.float32)).astype(jnp.bfloat16)
        both = jnp.dot(high, update[...], preferred_element_type=jnp.float32)
        both = both + jnp.dot(low, update[...], preferred_element_type=jnp.float32)
        added = both[:, :WIDTH] + both[:, WIDTH:]
        load(at).wait()
        blocks[at] = jnp.where(info[0] == 0, blocks[at], 0.0) + added

        @pl.when(has_top[at])
        def _():
            top_load.wait()
            blocks[at, 0:P_SIZE, :] = top_rows[...]

        store(at).start()
    for at in range(count):
        store(at).wait()


def apply_update(info, front, parts, update, top, done=None):
    vmem, hbm = pl.BlockSpec(memory_space=pltpu.VMEM), pl.BlockSpec(memory_space=pltpu.HBM)
    count = len(parts)
    front = pltpu.with_memory_space_constraint(front, pltpu.HBM)
    return pl.pallas_call(
        update_kernel,
        out_shape=jax.ShapeDtypeStruct((ROWS, WIDTH), jnp.float32),
        in_specs=[pl.BlockSpec(memory_space=pltpu.SMEM), hbm] + [vmem] * (count + 1) + [hbm] * (1 + (done is not None)),
        out_specs=hbm,
        scratch_shapes=[
            pltpu.VMEM((count, SHARE, WIDTH), jnp.float32),
            pltpu.VMEM((P_SIZE, WIDTH), jnp.float32),
            pltpu.SemaphoreType.DMA((count,)),
            pltpu.SemaphoreType.DMA((count,)),
            pltpu.SemaphoreType.DMA,
        ],
        input_output_aliases={} if done is None else {count + 4: 0},
        compiler_params=pltpu.CompilerParams(vmem_limit_bytes=4 << 20),
        cost_estimate=pl.CostEstimate(flops=3_000_000_000, bytes_accessed=4_000_000, transcendentals=0),
    )(info, front, *map(in_vmem, parts), in_vmem(update), pltpu.with_memory_space_constraint(top, pltpu.HBM), *([] if done is None else [done]))


def per_device(front):
    row, x, core, z, y = (lax.axis_index(a) for a in AXES)
    mine = coset(z, y)
    panel = (x == 0) & (z == 0) & (y < 2) & (core == 0)
    info = jnp.stack([core, panel.astype(jnp.int32), y, row]).astype(jnp.int32)

    def start(delta):
        return (mine + delta) % 4 * SHARE

    def rows(array, at, size=SHARE):
        return lax.dynamic_slice(array, (at, 0), (size, WIDTH))

    beside = send(front, CORE_SWAP)
    d_start = jnp.where(core == 0, front[:DPART], beside[DPART:P_SIZE])

    def share(delta):
        half = jnp.where(core == 0, rows(front, start(delta)), rows(beside, start(delta) + ROWS // 2))
        return jnp.concatenate([d_start, half])

    up = send(share(1), shift(1, 0))
    down = send(share(3), shift(-1, 0))
    side = send(share(2), SIDE)
    near = y < 2
    held = jnp.where((z == 1) & near, up, jnp.where((z == 3) & near, down, jnp.where(near, share(0), side)))
    held = jnp.where(x == 0, held, send(held, X_SWAP))

    role = member(z, y)
    part = jnp.where(role < 2, held, send(held, SPREAD))
    top_swapped = send(front[:P_SIZE], ROW_SWAP)
    top = jnp.where(row == 0, front[:P_SIZE], top_swapped)
    part, d_part = part[DPART:], part[:DPART]
    other = send(part, TRADE)
    d_part = jnp.where(row == 0, d_part, send(d_part, ROW_SWAP))
    d_traded = send(d_part, TRADE)

    def in_order(a, b):
        first = role % 2 == 0
        return jnp.stack([jnp.where(first, a, b), jnp.where(first, b, a)])

    own = in_order(part, other)
    d_mine = in_order(d_part, d_traded)
    before = send(own, shift(1, 0))
    after = send(own, shift(-1, 0))
    far = send(own, shift(0, 1))
    d_other = send(d_mine, CORE_SWAP)
    own_other = send(own, CORE_SWAP)
    update, top_done = factor(info, d_mine, d_other, top)

    order = [(mine + 3) % 4, (mine + 1) % 4, (mine + 2) % 4]

    def at(*blocks):
        return jnp.stack([panel.astype(jnp.int32), row, *blocks]).astype(jnp.int32)

    places = at(mine + 4 * core, mine + 4 * (1 - core))
    out = apply_update(places, front, (own, own_other), update, top_done)
    received = (before, after, far)
    others = tuple(send(v, CORE_SWAP) for v in received)
    places = at(*(p + 4 * core for p in order))
    out = apply_update(places, front, received, update, top_done, out)
    places = at(*(p + 4 * (1 - core) for p in order))
    return apply_update(places, front, others, update, top_done, out)


def solution(mesh):
    wide = jax.sharding.Mesh(mesh.devices.reshape(SHAPE), AXES)
    spec = P("row", ("x", "core", "z", "y"))

    return jax.shard_map(per_device, mesh=wide, in_specs=(spec,), out_specs=spec, check_vma=False)
```

```python
import jax
import jax.numpy as jnp
from jax import lax
from jax.experimental import pallas as pl
from jax.experimental.pallas import tpu as pltpu
from jax.sharding import PartitionSpec as P


B = 64
ITERS = 2
P_SIZE = 256

AXES = ("row", "x", "core", "z", "y")
SHAPE = (2, 2, 2, 4, 4)
ROWS = 4096
WIDTH = 128
SHARE = 512
DELTAS = (1, 3, 2, 0)
DPART = 128


def place(r, x, c, z, y):
    return (((r * 2 + x) * 2 + c) * 4 + z % 4) * 4 + y % 4


def everywhere(zy_pairs, xs=(0, 1)):
    return [
        (place(r, x, c, *a), place(r, x, c, *b)) for r in range(2) for x in xs for c in range(2) for a, b in zy_pairs
    ]


ALL_ZY = [(z, y) for z in range(4) for y in range(4)]


def shift(dz, dy):
    return everywhere([((z, y), (z + dz, y + dy)) for z, y in ALL_ZY])


ROW_DOWN = [(place(0, x, c, z, y), place(1, x, c, z, y)) for x in range(2) for c in range(2) for z, y in ALL_ZY]
CORE_SWAP = [
    (place(r, x, c, z, y), place(r, x, 1 - c, z, y)) for r in range(2) for x in range(2) for c in range(2) for z, y in ALL_ZY
]
X_SWAP = [
    (place(r, x, c, z, y), place(r, 1 - x, c, z, y)) for r in range(2) for x in range(2) for c in range(2) for z, y in ALL_ZY
]


def coset(z, y):
    return (z + 2 * y) % 4


SIDE = everywhere([((z, y), (z, 3 - y)) for z, y in ALL_ZY])
ROW_SWAP = ROW_DOWN + [(b, a) for a, b in ROW_DOWN]


def member(z, y):
    near = ((y == 0) & (z != 2)) | ((y == 3) & (z == 0))
    far = ((y == 1) & (z != 2)) | ((y == 2) & (z == 0))
    third = ((y == 2) & (z != 0)) | ((y == 1) & (z == 2))
    return 3 - 3 * near - 2 * far - third


def member_pairs():
    spread, trade = [], []
    for c in range(4):
        m = {int(member(z, y)): (z, y) for z, y in ALL_ZY if coset(z, y) == c}
        spread += [(m[0], m[2]), (m[1], m[3])]
        trade += [(m[0], m[1]), (m[1], m[0]), (m[2], m[3]), (m[3], m[2])]
    return everywhere(spread), everywhere(trade)


SPREAD, TRADE = member_pairs()


def send(value, pairs):
    return lax.ppermute(value, AXES, pairs)


def in_vmem(value):
    return pltpu.with_memory_space_constraint(value, pltpu.VMEM)


def payload_kernel(info, front, beside, *refs):
    outs, sems = refs[:-1], refs[-1]

    def copies(source, half):
        made = []
        for at, (delta, out) in enumerate(zip(DELTAS, outs)):
            begin = pl.multiple_of((info[1] + delta) % 4 * SHARE + half * (ROWS // 2), SHARE)
            pivots, rows = source.at[half * DPART : (half + 1) * DPART, :], source.at[pl.ds(begin, SHARE), :]
            made.append(pltpu.make_async_copy(pivots, out.at[0:DPART, :], sems.at[2 * at]))
            made.append(pltpu.make_async_copy(rows, out.at[DPART:, :], sems.at[2 * at + 1]))
        return made

    for half, source in enumerate((front, beside)):
        @pl.when(info[0] == half)
        def _():
            for copy in copies(source, half):
                copy.start()

    for copy in copies(front, 0):
        copy.wait()


def payloads(info, front, beside):
    hbm = pl.BlockSpec(memory_space=pltpu.HBM)
    front = pltpu.with_memory_space_constraint(front, pltpu.HBM)
    return pl.pallas_call(
        payload_kernel,
        out_shape=tuple(pltpu.VMEM((DPART + SHARE, WIDTH), jnp.float32) for _ in DELTAS),
        in_specs=[pl.BlockSpec(memory_space=pltpu.SMEM), hbm, pl.BlockSpec(memory_space=pltpu.VMEM)],
        out_specs=tuple(pl.BlockSpec(memory_space=pltpu.VMEM) for _ in DELTAS),
        scratch_shapes=[pltpu.SemaphoreType.DMA((2 * len(DELTAS),))],
        compiler_params=pltpu.CompilerParams(vmem_limit_bytes=4 << 20),
        name="payloads",
    )(info, front, in_vmem(beside))


def split3(value):
    high = value.astype(jnp.bfloat16)
    rest = value - high.astype(jnp.float32)
    middle = rest.astype(jnp.bfloat16)
    low = (rest - middle.astype(jnp.float32)).astype(jnp.bfloat16)
    return high, middle, low


def stacked_dot(left, right):
    lh, lm, ll = split3(left)
    rh, rm, rl = split3(right)
    lefts = jnp.concatenate([ll, lh, lm, lm, lh, lh], axis=1)
    rights = jnp.concatenate([rh, rl, rm, rh, rm, rh], axis=0)
    return jnp.dot(lefts, rights, preferred_element_type=jnp.float32)


def factor_kernel(info, d_mine, d_other, top, update_out, top_out, f, sem):
    core = info[0]
    kind = jnp.where(info[1] == 0, 0, info[2] + 1)
    sides = (slice(P_SIZE, P_SIZE + WIDTH), slice(0, WIDTH), slice(WIDTH, P_SIZE))
    for half in range(2):
        @pl.when(core == half)
        def _():
            for part in range(2):
                f[half * DPART : (half + 1) * DPART, part * WIDTH : (part + 1) * WIDTH] = d_mine[part]
                f[(1 - half) * DPART : (2 - half) * DPART, part * WIDTH : (part + 1) * WIDTH] = d_other[part]

    f[0:P_SIZE, P_SIZE:] = top[...]
    rows = lax.broadcasted_iota(jnp.int32, (P_SIZE, P_SIZE), 0)
    cols = lax.broadcasted_iota(jnp.int32, (P_SIZE, P_SIZE), 1)
    f[P_SIZE:, 0:P_SIZE] = jnp.where(rows == cols, 1.0, 0.0)
    f[P_SIZE:, P_SIZE:] = jnp.zeros((P_SIZE, WIDTH), jnp.float32)
    total = P_SIZE + WIDTH
    for block in range(P_SIZE // B):
        lo, hi = block * B, block * B + B
        base = lo // WIDTH * WIDTH
        r = lax.broadcasted_iota(jnp.int32, (WIDTH, WIDTH), 0) + base
        c = lax.broadcasted_iota(jnp.int32, (WIDTH, WIDTH), 1) + base
        in_block = (r >= lo) & (r < hi) & (c >= lo) & (c < hi)
        on_diag = in_block & (r == c)
        window = f[base : base + WIDTH, base : base + WIDTH]
        pivot = jnp.where(in_block, window, 0.0)
        diag = jnp.where(on_diag, window, 0.0)
        diag_row = jnp.sum(diag, axis=0, keepdims=True)
        diag_col = jnp.sum(diag, axis=1, keepdims=True)
        inv_row = 1.0 / jnp.where(diag_row == 0.0, 1.0, diag_row)
        inv_col = 1.0 / jnp.where(diag_col == 0.0, 1.0, diag_col)
        inverse = jnp.where(on_diag, 2.0 * inv_row, 0.0) - inv_col * (pivot * inv_row)
        for _ in range(ITERS - 1):
            inverse = 2.0 * inverse - stacked_dot(inverse, stacked_dot(pivot, inverse))
        lower = stacked_dot(f[hi:, base : base + WIDTH], inverse)
        left_col = hi // WIDTH * WIDTH
        col = lax.broadcasted_iota(jnp.int32, (WIDTH, total - left_col), 1) + left_col
        upper = jnp.where(col >= hi, f[base : base + WIDTH, left_col:], 0.0)
        f[hi:, left_col:] = f[hi:, left_col:] - stacked_dot(lower, upper)
        lane = lax.broadcasted_iota(jnp.int32, lower.shape, 1) + base
        mine = (lane >= lo) & (lane < hi)
        f[hi:, base : base + WIDTH] = jnp.where(mine, lower, f[hi:, base : base + WIDTH])
        if block == P_SIZE // B - 2:
            for case, side in enumerate(sides):
                @pl.when(kind == case)
                def _():
                    pltpu.make_async_copy(f.at[0:P_SIZE, side], top_out, sem).start()

    def finish(update):
        high = update.astype(jnp.bfloat16)
        low = (update - high.astype(jnp.float32)).astype(jnp.bfloat16)
        update_out[...] = jnp.concatenate([high, low], axis=1)

    for case, side in enumerate(sides):
        @pl.when(kind == case)
        def _():
            finish(f[P_SIZE:, side])

    pltpu.make_async_copy(f.at[0:P_SIZE, sides[0]], top_out, sem).wait()


def factor(info, d_mine, d_other, top):
    vmem = pl.BlockSpec(memory_space=pltpu.VMEM)
    return pl.pallas_call(
        factor_kernel,
        out_shape=(pltpu.VMEM((P_SIZE, 2 * WIDTH), jnp.bfloat16), pltpu.HBM((P_SIZE, WIDTH), jnp.float32)),
        in_specs=[pl.BlockSpec(memory_space=pltpu.SMEM), vmem, vmem, vmem],
        out_specs=(vmem, pl.BlockSpec(memory_space=pltpu.HBM)),
        scratch_shapes=[pltpu.VMEM((2 * P_SIZE, P_SIZE + WIDTH), jnp.float32), pltpu.SemaphoreType.DMA],
        compiler_params=pltpu.CompilerParams(vmem_limit_bytes=4 << 20),
        cost_estimate=pl.CostEstimate(flops=9_000_000_000, bytes_accessed=2_000_000, transcendentals=0),
        name="factor",
    )(info, in_vmem(d_mine), in_vmem(d_other), in_vmem(top))


def update_kernel(info, front, *refs):
    out, blocks, top_rows, loads, stores, top_sem = refs[-6:]
    count = blocks.shape[0]
    parts, update, top = refs[:count], refs[count], refs[count + 1]
    top_load = pltpu.make_async_copy(top, top_rows, top_sem)
    has_top = [(info[2 + at] == 0) & (info[1] == 0) for at in range(count)]

    def load(at):
        rows = pl.ds(pl.multiple_of(info[2 + at] * SHARE, SHARE), SHARE)
        return pltpu.make_async_copy(front.at[rows, :], blocks.at[at], loads.at[at])

    def store(at):
        rows = pl.ds(pl.multiple_of(info[2 + at] * SHARE, SHARE), SHARE)
        return pltpu.make_async_copy(blocks.at[at], out.at[rows, :], stores.at[at])

    for at in range(count):
        load(at).start()
        pl.when(has_top[at])(top_load.start)
    for at in range(count):
        panel = jnp.concatenate([parts[at][0], parts[at][1]], axis=1)
        high = panel.astype(jnp.bfloat16)
        low = (panel - high.astype(jnp.float32)).astype(jnp.bfloat16)
        both = jnp.dot(high, update[...], preferred_element_type=jnp.float32)
        both = both + jnp.dot(low, update[...], preferred_element_type=jnp.float32)
        added = both[:, :WIDTH] + both[:, WIDTH:]
        load(at).wait()
        blocks[at] = jnp.where(info[0] == 0, blocks[at], 0.0) + added

        @pl.when(has_top[at])
        def _():
            top_load.wait()
            blocks[at, 0:P_SIZE, :] = top_rows[...]

        store(at).start()
    for at in range(count):
        store(at).wait()


def apply_update(info, front, parts, update, top, done=None):
    vmem, hbm = pl.BlockSpec(memory_space=pltpu.VMEM), pl.BlockSpec(memory_space=pltpu.HBM)
    count = len(parts)
    front = pltpu.with_memory_space_constraint(front, pltpu.HBM)
    return pl.pallas_call(
        update_kernel,
        out_shape=jax.ShapeDtypeStruct((ROWS, WIDTH), jnp.float32),
        in_specs=[pl.BlockSpec(memory_space=pltpu.SMEM), hbm] + [vmem] * (count + 1) + [hbm] * (1 + (done is not None)),
        out_specs=hbm,
        scratch_shapes=[
            pltpu.VMEM((count, SHARE, WIDTH), jnp.float32),
            pltpu.VMEM((P_SIZE, WIDTH), jnp.float32),
            pltpu.SemaphoreType.DMA((count,)),
            pltpu.SemaphoreType.DMA((count,)),
            pltpu.SemaphoreType.DMA,
        ],
        input_output_aliases={} if done is None else {count + 4: 0},
        compiler_params=pltpu.CompilerParams(vmem_limit_bytes=4 << 20),
        cost_estimate=pl.CostEstimate(flops=3_000_000_000, bytes_accessed=4_000_000, transcendentals=0),
    )(info, front, *map(in_vmem, parts), in_vmem(update), pltpu.with_memory_space_constraint(top, pltpu.HBM), *([] if done is None else [done]))


def per_device(front):
    row, x, core, z, y = (lax.axis_index(a) for a in AXES)
    mine = coset(z, y)
    panel = (x == 0) & (z == 0) & (y < 2) & (core == 0)
    info = jnp.stack([core, panel.astype(jnp.int32), y, row]).astype(jnp.int32)

    beside = send(front, CORE_SWAP)
    to_up, to_down, to_side, to_self = payloads(jnp.stack([core, mine]).astype(jnp.int32), front, beside)
    up = send(to_up, shift(1, 0))
    down = send(to_down, shift(-1, 0))
    side = send(to_side, SIDE)
    near = y < 2
    held = jnp.where((z == 1) & near, up, jnp.where((z == 3) & near, down, jnp.where(near, to_self, side)))
    held = jnp.where(x == 0, held, send(held, X_SWAP))

    role = member(z, y)
    part = jnp.where(role < 2, held, send(held, SPREAD))
    top_swapped = send(front[:P_SIZE], ROW_SWAP)
    top = jnp.where(row == 0, front[:P_SIZE], top_swapped)
    part, d_part = part[DPART:], part[:DPART]
    other = send(part, TRADE)
    d_part = jnp.where(row == 0, d_part, send(d_part, ROW_SWAP))
    d_traded = send(d_part, TRADE)

    def in_order(a, b):
        first = role % 2 == 0
        return jnp.stack([jnp.where(first, a, b), jnp.where(first, b, a)])

    own = in_order(part, other)
    d_mine = in_order(d_part, d_traded)
    before = send(own, shift(1, 0))
    after = send(own, shift(-1, 0))
    far = send(own, shift(0, 1))
    d_other = send(d_mine, CORE_SWAP)
    own_other = send(own, CORE_SWAP)
    update, top_done = factor(info, d_mine, d_other, top)

    def at(*blocks):
        return jnp.stack([panel.astype(jnp.int32), row, *blocks]).astype(jnp.int32)

    here, there = core * 4, (1 - core) * 4
    earlier, later, middle = (mine + 3) % 4, (mine + 1) % 4, (mine + 2) % 4
    before_other = send(before, CORE_SWAP)
    places = at(mine + here, mine + there, earlier + here)
    out = apply_update(places, front, (own, own_other, before), update, top_done)
    after_other, far_other = send(after, CORE_SWAP), send(far, CORE_SWAP)
    places = at(later + here, middle + here, earlier + there)
    out = apply_update(places, front, (after, far, before_other), update, top_done, out)
    places = at(later + there, middle + there)
    return apply_update(places, front, (after_other, far_other), update, top_done, out)


def solution(mesh):
    wide = jax.sharding.Mesh(mesh.devices.reshape(SHAPE), AXES)
    spec = P("row", ("x", "core", "z", "y"))

    return jax.shard_map(per_device, mesh=wide, in_specs=(spec,), out_specs=spec, check_vma=False)
```

```python
import jax
import jax.numpy as jnp
from jax import lax
from jax.experimental import pallas as pl
from jax.experimental.pallas import tpu as pltpu
from jax.sharding import PartitionSpec as P


B = 64
ITERS = 2
P_SIZE = 256

AXES = ("row", "x", "core", "z", "y")
SHAPE = (2, 2, 2, 4, 4)
ROWS = 4096
WIDTH = 128
SHARE = 512
DELTAS = (1, 3, 2, 0)
DPART = 128


def place(r, x, c, z, y):
    return (((r * 2 + x) * 2 + c) * 4 + z % 4) * 4 + y % 4


def everywhere(zy_pairs, xs=(0, 1)):
    return [
        (place(r, x, c, *a), place(r, x, c, *b)) for r in range(2) for x in xs for c in range(2) for a, b in zy_pairs
    ]


ALL_ZY = [(z, y) for z in range(4) for y in range(4)]


def shift(dz, dy):
    return everywhere([((z, y), (z + dz, y + dy)) for z, y in ALL_ZY])


ROW_DOWN = [(place(0, x, c, z, y), place(1, x, c, z, y)) for x in range(2) for c in range(2) for z, y in ALL_ZY]
CORE_SWAP = [
    (place(r, x, c, z, y), place(r, x, 1 - c, z, y)) for r in range(2) for x in range(2) for c in range(2) for z, y in ALL_ZY
]
X_SWAP = [
    (place(r, x, c, z, y), place(r, 1 - x, c, z, y)) for r in range(2) for x in range(2) for c in range(2) for z, y in ALL_ZY
]


def coset(z, y):
    return (z + 2 * y) % 4


SIDE = everywhere([((z, y), (z, 3 - y)) for z, y in ALL_ZY])
ROW_SWAP = ROW_DOWN + [(b, a) for a, b in ROW_DOWN]


def member(z, y):
    near = ((y == 0) & (z != 2)) | ((y == 3) & (z == 0))
    far = ((y == 1) & (z != 2)) | ((y == 2) & (z == 0))
    third = ((y == 2) & (z != 0)) | ((y == 1) & (z == 2))
    return 3 - 3 * near - 2 * far - third


def member_pairs():
    spread, trade = [], []
    for c in range(4):
        m = {int(member(z, y)): (z, y) for z, y in ALL_ZY if coset(z, y) == c}
        spread += [(m[0], m[2]), (m[1], m[3])]
        trade += [(m[0], m[1]), (m[1], m[0]), (m[2], m[3]), (m[3], m[2])]
    return everywhere(spread), everywhere(trade)


SPREAD, TRADE = member_pairs()


def send(value, pairs):
    return lax.ppermute(value, AXES, pairs)


def in_vmem(value):
    return pltpu.with_memory_space_constraint(value, pltpu.VMEM)


def payload_kernel(info, front, *refs):
    outs, sems = refs[:-1], refs[-1]
    made = []
    for at, out in enumerate(outs):
        delta, half = DELTAS[at // 2], at % 2
        begin = pl.multiple_of((info[0] + delta) % 4 * SHARE + half * (ROWS // 2), SHARE)
        pivots, rows = front.at[half * DPART : (half + 1) * DPART, :], front.at[pl.ds(begin, SHARE), :]
        made.append(pltpu.make_async_copy(pivots, out.at[0:DPART, :], sems.at[2 * at]))
        made.append(pltpu.make_async_copy(rows, out.at[DPART:, :], sems.at[2 * at + 1]))
    for copy in made:
        copy.start()
    for copy in made:
        copy.wait()


def payloads(info, front):
    count = 2 * len(DELTAS)
    front = pltpu.with_memory_space_constraint(front, pltpu.HBM)
    out = pl.pallas_call(
        payload_kernel,
        out_shape=tuple(pltpu.VMEM((DPART + SHARE, WIDTH), jnp.float32) for _ in range(count)),
        in_specs=[pl.BlockSpec(memory_space=pltpu.SMEM), pl.BlockSpec(memory_space=pltpu.HBM)],
        out_specs=tuple(pl.BlockSpec(memory_space=pltpu.VMEM) for _ in range(count)),
        scratch_shapes=[pltpu.SemaphoreType.DMA((2 * count,))],
        compiler_params=pltpu.CompilerParams(vmem_limit_bytes=4 << 20),
        name="payloads",
    )(info, front)
    return out[0::2], out[1::2]


def split3(value):
    high = value.astype(jnp.bfloat16)
    rest = value - high.astype(jnp.float32)
    middle = rest.astype(jnp.bfloat16)
    low = (rest - middle.astype(jnp.float32)).astype(jnp.bfloat16)
    return high, middle, low


def stacked_dot(left, right):
    lh, lm, ll = split3(left)
    rh, rm, rl = split3(right)
    lefts = jnp.concatenate([ll, lh, lm, lm, lh, lh], axis=1)
    rights = jnp.concatenate([rh, rl, rm, rh, rm, rh], axis=0)
    return jnp.dot(lefts, rights, preferred_element_type=jnp.float32)


def factor_kernel(info, d_mine, d_other, top, update_out, top_out, f, sem):
    core = info[0]
    kind = jnp.where(info[1] == 0, 0, info[2] + 1)
    sides = (slice(P_SIZE, P_SIZE + WIDTH), slice(0, WIDTH), slice(WIDTH, P_SIZE))
    for half in range(2):
        @pl.when(core == half)
        def _():
            for part in range(2):
                f[half * DPART : (half + 1) * DPART, part * WIDTH : (part + 1) * WIDTH] = d_mine[part]
                f[(1 - half) * DPART : (2 - half) * DPART, part * WIDTH : (part + 1) * WIDTH] = d_other[part]

    f[0:P_SIZE, P_SIZE:] = top[...]
    rows = lax.broadcasted_iota(jnp.int32, (P_SIZE, P_SIZE), 0)
    cols = lax.broadcasted_iota(jnp.int32, (P_SIZE, P_SIZE), 1)
    f[P_SIZE:, 0:P_SIZE] = jnp.where(rows == cols, 1.0, 0.0)
    f[P_SIZE:, P_SIZE:] = jnp.zeros((P_SIZE, WIDTH), jnp.float32)
    total = P_SIZE + WIDTH
    for block in range(P_SIZE // B):
        lo, hi = block * B, block * B + B
        base = lo // WIDTH * WIDTH
        r = lax.broadcasted_iota(jnp.int32, (WIDTH, WIDTH), 0) + base
        c = lax.broadcasted_iota(jnp.int32, (WIDTH, WIDTH), 1) + base
        in_block = (r >= lo) & (r < hi) & (c >= lo) & (c < hi)
        on_diag = in_block & (r == c)
        window = f[base : base + WIDTH, base : base + WIDTH]
        pivot = jnp.where(in_block, window, 0.0)
        diag = jnp.where(on_diag, window, 0.0)
        diag_row = jnp.sum(diag, axis=0, keepdims=True)
        diag_col = jnp.sum(diag, axis=1, keepdims=True)
        inv_row = 1.0 / jnp.where(diag_row == 0.0, 1.0, diag_row)
        inv_col = 1.0 / jnp.where(diag_col == 0.0, 1.0, diag_col)
        inverse = jnp.where(on_diag, 2.0 * inv_row, 0.0) - inv_col * (pivot * inv_row)
        for _ in range(ITERS - 1):
            inverse = 2.0 * inverse - stacked_dot(inverse, stacked_dot(pivot, inverse))
        lower = stacked_dot(f[hi:, base : base + WIDTH], inverse)
        left_col = hi // WIDTH * WIDTH
        col = lax.broadcasted_iota(jnp.int32, (WIDTH, total - left_col), 1) + left_col
        upper = jnp.where(col >= hi, f[base : base + WIDTH, left_col:], 0.0)
        f[hi:, left_col:] = f[hi:, left_col:] - stacked_dot(lower, upper)
        lane = lax.broadcasted_iota(jnp.int32, lower.shape, 1) + base
        mine = (lane >= lo) & (lane < hi)
        f[hi:, base : base + WIDTH] = jnp.where(mine, lower, f[hi:, base : base + WIDTH])
        if block == P_SIZE // B - 2:
            for case, side in enumerate(sides):
                @pl.when(kind == case)
                def _():
                    pltpu.make_async_copy(f.at[0:P_SIZE, side], top_out, sem).start()

    def finish(update):
        high = update.astype(jnp.bfloat16)
        low = (update - high.astype(jnp.float32)).astype(jnp.bfloat16)
        update_out[...] = jnp.concatenate([high, low], axis=1)

    for case, side in enumerate(sides):
        @pl.when(kind == case)
        def _():
            finish(f[P_SIZE:, side])

    pltpu.make_async_copy(f.at[0:P_SIZE, sides[0]], top_out, sem).wait()


def factor(info, d_mine, d_other, top):
    vmem = pl.BlockSpec(memory_space=pltpu.VMEM)
    return pl.pallas_call(
        factor_kernel,
        out_shape=(pltpu.VMEM((P_SIZE, 2 * WIDTH), jnp.bfloat16), pltpu.HBM((P_SIZE, WIDTH), jnp.float32)),
        in_specs=[pl.BlockSpec(memory_space=pltpu.SMEM), vmem, vmem, vmem],
        out_specs=(vmem, pl.BlockSpec(memory_space=pltpu.HBM)),
        scratch_shapes=[pltpu.VMEM((2 * P_SIZE, P_SIZE + WIDTH), jnp.float32), pltpu.SemaphoreType.DMA],
        compiler_params=pltpu.CompilerParams(vmem_limit_bytes=4 << 20),
        cost_estimate=pl.CostEstimate(flops=9_000_000_000, bytes_accessed=2_000_000, transcendentals=0),
        name="factor",
    )(info, in_vmem(d_mine), in_vmem(d_other), in_vmem(top))


def update_kernel(info, front, *refs):
    out, blocks, top_rows, loads, stores, top_sem = refs[-6:]
    count = blocks.shape[0]
    parts, update, top = refs[:count], refs[count], refs[count + 1]
    top_load = pltpu.make_async_copy(top, top_rows, top_sem)
    has_top = [(info[2 + at] == 0) & (info[1] == 0) for at in range(count)]

    def load(at):
        rows = pl.ds(pl.multiple_of(info[2 + at] * SHARE, SHARE), SHARE)
        return pltpu.make_async_copy(front.at[rows, :], blocks.at[at], loads.at[at])

    def store(at):
        rows = pl.ds(pl.multiple_of(info[2 + at] * SHARE, SHARE), SHARE)
        return pltpu.make_async_copy(blocks.at[at], out.at[rows, :], stores.at[at])

    for at in range(count):
        load(at).start()
        pl.when(has_top[at])(top_load.start)
    for at in range(count):
        panel = jnp.concatenate([parts[at][0], parts[at][1]], axis=1)
        high = panel.astype(jnp.bfloat16)
        low = (panel - high.astype(jnp.float32)).astype(jnp.bfloat16)
        both = jnp.dot(high, update[...], preferred_element_type=jnp.float32)
        both = both + jnp.dot(low, update[...], preferred_element_type=jnp.float32)
        added = both[:, :WIDTH] + both[:, WIDTH:]
        load(at).wait()
        blocks[at] = jnp.where(info[0] == 0, blocks[at], 0.0) + added

        @pl.when(has_top[at])
        def _():
            top_load.wait()
            blocks[at, 0:P_SIZE, :] = top_rows[...]

        store(at).start()
    for at in range(count):
        store(at).wait()


def apply_update(info, front, parts, update, top, done=None):
    vmem, hbm = pl.BlockSpec(memory_space=pltpu.VMEM), pl.BlockSpec(memory_space=pltpu.HBM)
    count = len(parts)
    front = pltpu.with_memory_space_constraint(front, pltpu.HBM)
    return pl.pallas_call(
        update_kernel,
        out_shape=jax.ShapeDtypeStruct((ROWS, WIDTH), jnp.float32),
        in_specs=[pl.BlockSpec(memory_space=pltpu.SMEM), hbm] + [vmem] * (count + 1) + [hbm] * (1 + (done is not None)),
        out_specs=hbm,
        scratch_shapes=[
            pltpu.VMEM((count, SHARE, WIDTH), jnp.float32),
            pltpu.VMEM((P_SIZE, WIDTH), jnp.float32),
            pltpu.SemaphoreType.DMA((count,)),
            pltpu.SemaphoreType.DMA((count,)),
            pltpu.SemaphoreType.DMA,
        ],
        input_output_aliases={} if done is None else {count + 4: 0},
        compiler_params=pltpu.CompilerParams(vmem_limit_bytes=4 << 20),
        cost_estimate=pl.CostEstimate(flops=3_000_000_000, bytes_accessed=4_000_000, transcendentals=0),
    )(info, front, *map(in_vmem, parts), in_vmem(update), pltpu.with_memory_space_constraint(top, pltpu.HBM), *([] if done is None else [done]))


def per_device(front):
    row, x, core, z, y = (lax.axis_index(a) for a in AXES)
    mine = coset(z, y)
    panel = (x == 0) & (z == 0) & (y < 2) & (core == 0)
    info = jnp.stack([core, panel.astype(jnp.int32), y, row]).astype(jnp.int32)

    kept, given = payloads(mine.reshape(1).astype(jnp.int32), front)

    def payload(at):
        return jnp.where(core == 0, kept[at], send(given[at], CORE_SWAP))

    up = send(payload(0), shift(1, 0))
    down = send(payload(1), shift(-1, 0))
    side = send(payload(2), SIDE)
    to_self = payload(3)
    near = y < 2
    held = jnp.where((z == 1) & near, up, jnp.where((z == 3) & near, down, jnp.where(near, to_self, side)))
    held = jnp.where(x == 0, held, send(held, X_SWAP))

    role = member(z, y)
    part = jnp.where(role < 2, held, send(held, SPREAD))
    top_swapped = send(front[:P_SIZE], ROW_SWAP)
    top = jnp.where(row == 0, front[:P_SIZE], top_swapped)
    part, d_part = part[DPART:], part[:DPART]
    other = send(part, TRADE)
    d_part = jnp.where(row == 0, d_part, send(d_part, ROW_SWAP))
    d_traded = send(d_part, TRADE)

    def in_order(a, b):
        first = role % 2 == 0
        return jnp.stack([jnp.where(first, a, b), jnp.where(first, b, a)])

    own = in_order(part, other)
    d_mine = in_order(d_part, d_traded)
    before = send(own, shift(1, 0))
    after = send(own, shift(-1, 0))
    far = send(own, shift(0, 1))
    d_other = send(d_mine, CORE_SWAP)
    own_other = send(own, CORE_SWAP)
    update, top_done = factor(info, d_mine, d_other, top)

    def at(*blocks):
        return jnp.stack([panel.astype(jnp.int32), row, *blocks]).astype(jnp.int32)

    here, there = core * 4, (1 - core) * 4
    earlier, later, middle = (mine + 3) % 4, (mine + 1) % 4, (mine + 2) % 4
    before_other = send(before, CORE_SWAP)
    places = at(mine + here, mine + there, earlier + here)
    out = apply_update(places, front, (own, own_other, before), update, top_done)
    after_other, far_other = send(after, CORE_SWAP), send(far, CORE_SWAP)
    places = at(later + here, middle + here, earlier + there)
    out = apply_update(places, front, (after, far, before_other), update, top_done, out)
    places = at(later + there, middle + there)
    return apply_update(places, front, (after_other, far_other), update, top_done, out)


def solution(mesh):
    wide = jax.sharding.Mesh(mesh.devices.reshape(SHAPE), AXES)
    spec = P("row", ("x", "core", "z", "y"))

    return jax.shard_map(per_device, mesh=wide, in_specs=(spec,), out_specs=spec, check_vma=False)
```

```python
import jax
import jax.numpy as jnp
from jax import lax
from jax.experimental import pallas as pl
from jax.experimental.pallas import tpu as pltpu
from jax.sharding import PartitionSpec as P


B = 64
ITERS = 2
P_SIZE = 256

AXES = ("row", "x", "core", "z", "y")
SHAPE = (2, 2, 2, 4, 4)
ROWS = 4096
WIDTH = 128
SHARE = 512
DELTAS = (1, 3, 2, 0)
DPART = 128


def place(r, x, c, z, y):
    return (((r * 2 + x) * 2 + c) * 4 + z % 4) * 4 + y % 4


def everywhere(zy_pairs, xs=(0, 1)):
    return [
        (place(r, x, c, *a), place(r, x, c, *b)) for r in range(2) for x in xs for c in range(2) for a, b in zy_pairs
    ]


ALL_ZY = [(z, y) for z in range(4) for y in range(4)]


def shift(dz, dy):
    return everywhere([((z, y), (z + dz, y + dy)) for z, y in ALL_ZY])


ROW_DOWN = [(place(0, x, c, z, y), place(1, x, c, z, y)) for x in range(2) for c in range(2) for z, y in ALL_ZY]
CORE_SWAP = [
    (place(r, x, c, z, y), place(r, x, 1 - c, z, y)) for r in range(2) for x in range(2) for c in range(2) for z, y in ALL_ZY
]
X_SWAP = [
    (place(r, x, c, z, y), place(r, 1 - x, c, z, y)) for r in range(2) for x in range(2) for c in range(2) for z, y in ALL_ZY
]


def coset(z, y):
    return (z + 2 * y) % 4


SIDE = everywhere([((z, y), (z, 3 - y)) for z, y in ALL_ZY])
ROW_SWAP = ROW_DOWN + [(b, a) for a, b in ROW_DOWN]


def member(z, y):
    near = ((y == 0) & (z != 2)) | ((y == 3) & (z == 0))
    far = ((y == 1) & (z != 2)) | ((y == 2) & (z == 0))
    third = ((y == 2) & (z != 0)) | ((y == 1) & (z == 2))
    return 3 - 3 * near - 2 * far - third


def member_pairs():
    spread, trade = [], []
    for c in range(4):
        m = {int(member(z, y)): (z, y) for z, y in ALL_ZY if coset(z, y) == c}
        spread += [(m[0], m[2]), (m[1], m[3]), (m[2], m[0]), (m[3], m[1])]
        trade += [(m[0], m[1]), (m[1], m[0]), (m[2], m[3]), (m[3], m[2])]
    return everywhere(spread), everywhere(trade)


SPREAD, TRADE = member_pairs()


def send(value, pairs):
    return lax.ppermute(value, AXES, pairs)


def in_vmem(value):
    return pltpu.with_memory_space_constraint(value, pltpu.VMEM)


def payload_kernel(info, front, beside, *refs):
    outs, sems = refs[:-1], refs[-1]

    def copies(source, half):
        made = []
        for at, (delta, out) in enumerate(zip(DELTAS, outs)):
            begin = pl.multiple_of((info[1] + delta) % 4 * SHARE + half * (ROWS // 2), SHARE)
            pivots, rows = source.at[half * DPART : (half + 1) * DPART, :], source.at[pl.ds(begin, SHARE), :]
            made.append(pltpu.make_async_copy(pivots, out.at[0:DPART, :], sems.at[2 * at]))
            made.append(pltpu.make_async_copy(rows, out.at[DPART:, :], sems.at[2 * at + 1]))
        return made

    for half, source in enumerate((front, beside)):
        @pl.when(info[0] == half)
        def _():
            for copy in copies(source, half):
                copy.start()

    for copy in copies(front, 0):
        copy.wait()


def payloads(info, front, beside):
    hbm = pl.BlockSpec(memory_space=pltpu.HBM)
    front = pltpu.with_memory_space_constraint(front, pltpu.HBM)
    return pl.pallas_call(
        payload_kernel,
        out_shape=tuple(pltpu.VMEM((DPART + SHARE, WIDTH), jnp.float32) for _ in DELTAS),
        in_specs=[pl.BlockSpec(memory_space=pltpu.SMEM), hbm, pl.BlockSpec(memory_space=pltpu.VMEM)],
        out_specs=tuple(pl.BlockSpec(memory_space=pltpu.VMEM) for _ in DELTAS),
        scratch_shapes=[pltpu.SemaphoreType.DMA((2 * len(DELTAS),))],
        compiler_params=pltpu.CompilerParams(vmem_limit_bytes=4 << 20),
        name="payloads",
    )(info, front, in_vmem(beside))


def split3(value):
    high = value.astype(jnp.bfloat16)
    rest = value - high.astype(jnp.float32)
    middle = rest.astype(jnp.bfloat16)
    low = (rest - middle.astype(jnp.float32)).astype(jnp.bfloat16)
    return high, middle, low


def stacked_dot(left, right):
    lh, lm, ll = split3(left)
    rh, rm, rl = split3(right)
    lefts = jnp.concatenate([ll, lh, lm, lm, lh, lh], axis=1)
    rights = jnp.concatenate([rh, rl, rm, rh, rm, rh], axis=0)
    return jnp.dot(lefts, rights, preferred_element_type=jnp.float32)


def factor_kernel(info, d_mine, d_other, top, update_out, top_out, f, sem):
    core = info[0]
    kind = jnp.where(info[1] == 0, 0, info[2] + 1)
    sides = (slice(P_SIZE, P_SIZE + WIDTH), slice(0, WIDTH), slice(WIDTH, P_SIZE))
    for half in range(2):
        @pl.when(core == half)
        def _():
            for part in range(2):
                f[half * DPART : (half + 1) * DPART, part * WIDTH : (part + 1) * WIDTH] = d_mine[part]
                f[(1 - half) * DPART : (2 - half) * DPART, part * WIDTH : (part + 1) * WIDTH] = d_other[part]

    f[0:P_SIZE, P_SIZE:] = top[...]
    rows = lax.broadcasted_iota(jnp.int32, (P_SIZE, P_SIZE), 0)
    cols = lax.broadcasted_iota(jnp.int32, (P_SIZE, P_SIZE), 1)
    f[P_SIZE:, 0:P_SIZE] = jnp.where(rows == cols, 1.0, 0.0)
    f[P_SIZE:, P_SIZE:] = jnp.zeros((P_SIZE, WIDTH), jnp.float32)
    total = P_SIZE + WIDTH
    for block in range(P_SIZE // B):
        lo, hi = block * B, block * B + B
        base = lo // WIDTH * WIDTH
        r = lax.broadcasted_iota(jnp.int32, (WIDTH, WIDTH), 0) + base
        c = lax.broadcasted_iota(jnp.int32, (WIDTH, WIDTH), 1) + base
        in_block = (r >= lo) & (r < hi) & (c >= lo) & (c < hi)
        on_diag = in_block & (r == c)
        window = f[base : base + WIDTH, base : base + WIDTH]
        pivot = jnp.where(in_block, window, 0.0)
        diag = jnp.where(on_diag, window, 0.0)
        diag_row = jnp.sum(diag, axis=0, keepdims=True)
        diag_col = jnp.sum(diag, axis=1, keepdims=True)
        inv_row = 1.0 / jnp.where(diag_row == 0.0, 1.0, diag_row)
        inv_col = 1.0 / jnp.where(diag_col == 0.0, 1.0, diag_col)
        inverse = jnp.where(on_diag, 2.0 * inv_row, 0.0) - inv_col * (pivot * inv_row)
        for _ in range(ITERS - 1):
            inverse = 2.0 * inverse - stacked_dot(inverse, stacked_dot(pivot, inverse))
        lower = stacked_dot(f[hi:, base : base + WIDTH], inverse)
        left_col = hi // WIDTH * WIDTH
        col = lax.broadcasted_iota(jnp.int32, (WIDTH, total - left_col), 1) + left_col
        upper = jnp.where(col >= hi, f[base : base + WIDTH, left_col:], 0.0)
        f[hi:, left_col:] = f[hi:, left_col:] - stacked_dot(lower, upper)
        lane = lax.broadcasted_iota(jnp.int32, lower.shape, 1) + base
        mine = (lane >= lo) & (lane < hi)
        f[hi:, base : base + WIDTH] = jnp.where(mine, lower, f[hi:, base : base + WIDTH])
        if block == P_SIZE // B - 2:
            for case, side in enumerate(sides):
                @pl.when(kind == case)
                def _():
                    pltpu.make_async_copy(f.at[0:P_SIZE, side], top_out, sem).start()

    def finish(update):
        high = update.astype(jnp.bfloat16)
        low = (update - high.astype(jnp.float32)).astype(jnp.bfloat16)
        both = jnp.concatenate([high, low], axis=1)
        update_out[...] = jnp.concatenate([both, both], axis=0)

    for case, side in enumerate(sides):
        @pl.when(kind == case)
        def _():
            finish(f[P_SIZE:, side])

    pltpu.make_async_copy(f.at[0:P_SIZE, sides[0]], top_out, sem).wait()


def factor(info, d_mine, d_other, top):
    vmem = pl.BlockSpec(memory_space=pltpu.VMEM)
    return pl.pallas_call(
        factor_kernel,
        out_shape=(pltpu.VMEM((2 * P_SIZE, 2 * WIDTH), jnp.bfloat16), pltpu.HBM((P_SIZE, WIDTH), jnp.float32)),
        in_specs=[pl.BlockSpec(memory_space=pltpu.SMEM), vmem, vmem, vmem],
        out_specs=(vmem, pl.BlockSpec(memory_space=pltpu.HBM)),
        scratch_shapes=[pltpu.VMEM((2 * P_SIZE, P_SIZE + WIDTH), jnp.float32), pltpu.SemaphoreType.DMA],
        compiler_params=pltpu.CompilerParams(vmem_limit_bytes=4 << 20),
        cost_estimate=pl.CostEstimate(flops=9_000_000_000, bytes_accessed=2_000_000, transcendentals=0),
        name="factor",
    )(info, in_vmem(d_mine), in_vmem(d_other), in_vmem(top))


def update_kernel(info, front, *refs):
    out, blocks, top_rows, loads, stores, top_sem = refs[-6:]
    count = blocks.shape[0]
    parts, update, top = refs[:count], refs[count], refs[count + 1]
    top_load = pltpu.make_async_copy(top, top_rows, top_sem)
    has_top = [(info[2 + at] == 0) & (info[1] == 0) for at in range(count)]

    def load(at):
        rows = pl.ds(pl.multiple_of(info[2 + at] * SHARE, SHARE), SHARE)
        return pltpu.make_async_copy(front.at[rows, :], blocks.at[at], loads.at[at])

    def store(at, half):
        begin = pl.multiple_of(info[2 + at] * SHARE + half * P_SIZE, P_SIZE)
        mine = blocks.at[at, half * P_SIZE : (half + 1) * P_SIZE, :]
        return pltpu.make_async_copy(mine, out.at[pl.ds(begin, P_SIZE), :], stores.at[at, half])

    for at in range(count):
        load(at).start()
        pl.when(has_top[at])(top_load.start)
    for at in range(count):
        for half in range(2):
            rows = slice(half * P_SIZE, (half + 1) * P_SIZE)
            panel = jnp.concatenate([parts[at][0, rows, :], parts[at][1, rows, :]], axis=1)
            high = panel.astype(jnp.bfloat16)
            low = (panel - high.astype(jnp.float32)).astype(jnp.bfloat16)
            both = jnp.dot(jnp.concatenate([high, low], axis=1), update[...], preferred_element_type=jnp.float32)
            added = both[:, :WIDTH] + both[:, WIDTH:]
            if half == 0:
                load(at).wait()
            blocks[at, rows, :] = jnp.where(info[0] == 0, blocks[at, rows, :], 0.0) + added
            if half == 0:
                @pl.when(has_top[at])
                def _():
                    top_load.wait()
                    blocks[at, 0:P_SIZE, :] = top_rows[...]

            store(at, half).start()
    for at in range(count):
        for half in range(2):
            store(at, half).wait()


def apply_update(info, front, parts, update, top, done=None):
    vmem, hbm = pl.BlockSpec(memory_space=pltpu.VMEM), pl.BlockSpec(memory_space=pltpu.HBM)
    count = len(parts)
    front = pltpu.with_memory_space_constraint(front, pltpu.HBM)
    return pl.pallas_call(
        update_kernel,
        out_shape=jax.ShapeDtypeStruct((ROWS, WIDTH), jnp.float32),
        in_specs=[pl.BlockSpec(memory_space=pltpu.SMEM), hbm] + [vmem] * (count + 1) + [hbm] * (1 + (done is not None)),
        out_specs=hbm,
        scratch_shapes=[
            pltpu.VMEM((count, SHARE, WIDTH), jnp.float32),
            pltpu.VMEM((P_SIZE, WIDTH), jnp.float32),
            pltpu.SemaphoreType.DMA((count,)),
            pltpu.SemaphoreType.DMA((count, 2)),
            pltpu.SemaphoreType.DMA,
        ],
        input_output_aliases={} if done is None else {count + 4: 0},
        compiler_params=pltpu.CompilerParams(vmem_limit_bytes=4 << 20),
        cost_estimate=pl.CostEstimate(flops=3_000_000_000, bytes_accessed=4_000_000, transcendentals=0),
    )(info, front, *map(in_vmem, parts), in_vmem(update), pltpu.with_memory_space_constraint(top, pltpu.HBM), *([] if done is None else [done]))


def per_device(front):
    row, x, core, z, y = (lax.axis_index(a) for a in AXES)
    mine = coset(z, y)
    panel = (x == 0) & (z == 0) & (y < 2) & (core == 0)
    info = jnp.stack([core, panel.astype(jnp.int32), y, row]).astype(jnp.int32)

    beside = send(front, CORE_SWAP)
    to_up, to_down, to_side, to_self = payloads(jnp.stack([core, mine]).astype(jnp.int32), front, beside)
    up = send(to_up, shift(1, 0))
    down = send(to_down, shift(-1, 0))
    side = send(to_side, SIDE)
    near = y < 2
    held = jnp.where((z == 1) & near, up, jnp.where((z == 3) & near, down, jnp.where(near, to_self, side)))
    held = jnp.where(x == 0, held, send(held, X_SWAP))

    role = member(z, y)
    part = jnp.where(role < 2, held, send(held, SPREAD))
    top_swapped = send(front[:P_SIZE], ROW_SWAP)
    top = jnp.where(row == 0, front[:P_SIZE], top_swapped)
    part, d_part = part[DPART:], part[:DPART]
    other = send(part, TRADE)
    d_part = jnp.where(row == 0, d_part, send(d_part, ROW_SWAP))
    d_traded = send(d_part, TRADE)

    def in_order(a, b):
        first = role % 2 == 0
        return jnp.stack([jnp.where(first, a, b), jnp.where(first, b, a)])

    own = in_order(part, other)
    d_mine = in_order(d_part, d_traded)
    before = send(own, shift(1, 0))
    after = send(own, shift(-1, 0))
    far = send(own, shift(0, 1))
    d_other = send(d_mine, CORE_SWAP)
    own_other = send(own, CORE_SWAP)
    update, top_done = factor(info, d_mine, d_other, top)

    def at(*blocks):
        return jnp.stack([panel.astype(jnp.int32), row, *blocks]).astype(jnp.int32)

    here, there = core * 4, (1 - core) * 4
    earlier, later, middle = (mine + 3) % 4, (mine + 1) % 4, (mine + 2) % 4
    before_other = send(before, CORE_SWAP)
    places = at(mine + here, mine + there, earlier + here)
    out = apply_update(places, front, (own, own_other, before), update, top_done)
    after_other, far_other = send(after, CORE_SWAP), send(far, CORE_SWAP)
    places = at(later + here, middle + here, earlier + there)
    out = apply_update(places, front, (after, far, before_other), update, top_done, out)
    places = at(later + there, middle + there)
    return apply_update(places, front, (after_other, far_other), update, top_done, out)


def solution(mesh):
    wide = jax.sharding.Mesh(mesh.devices.reshape(SHAPE), AXES)
    spec = P("row", ("x", "core", "z", "y"))

    return jax.shard_map(per_device, mesh=wide, in_specs=(spec,), out_specs=spec, check_vma=False)
```

```python
import jax
import jax.numpy as jnp
from jax import lax
from jax.experimental import pallas as pl
from jax.experimental.pallas import tpu as pltpu
from jax.sharding import PartitionSpec as P


B = 64
ITERS = 2
P_SIZE = 256

AXES = ("row", "x", "core", "z", "y")
SHAPE = (2, 2, 2, 4, 4)
ROWS = 4096
WIDTH = 128
SHARE = 512
DELTAS = (1, 3, 2, 0)
DPART = 128


def place(r, x, c, z, y):
    return (((r * 2 + x) * 2 + c) * 4 + z % 4) * 4 + y % 4


def everywhere(zy_pairs, xs=(0, 1)):
    return [
        (place(r, x, c, *a), place(r, x, c, *b)) for r in range(2) for x in xs for c in range(2) for a, b in zy_pairs
    ]


ALL_ZY = [(z, y) for z in range(4) for y in range(4)]


def shift(dz, dy):
    return everywhere([((z, y), (z + dz, y + dy)) for z, y in ALL_ZY])


ROW_DOWN = [(place(0, x, c, z, y), place(1, x, c, z, y)) for x in range(2) for c in range(2) for z, y in ALL_ZY]
CORE_SWAP = [
    (place(r, x, c, z, y), place(r, x, 1 - c, z, y)) for r in range(2) for x in range(2) for c in range(2) for z, y in ALL_ZY
]
X_SWAP = [
    (place(r, x, c, z, y), place(r, 1 - x, c, z, y)) for r in range(2) for x in range(2) for c in range(2) for z, y in ALL_ZY
]


def coset(z, y):
    return (z + 2 * y) % 4


SIDE = everywhere([((z, y), (z, 3 - y)) for z, y in ALL_ZY])
ROW_SWAP = ROW_DOWN + [(b, a) for a, b in ROW_DOWN]


def member(z, y):
    near = ((y == 0) & (z != 2)) | ((y == 3) & (z == 0))
    far = ((y == 1) & (z != 2)) | ((y == 2) & (z == 0))
    third = ((y == 2) & (z != 0)) | ((y == 1) & (z == 2))
    return 3 - 3 * near - 2 * far - third


def member_pairs():
    spread, trade = [], []
    for c in range(4):
        m = {int(member(z, y)): (z, y) for z, y in ALL_ZY if coset(z, y) == c}
        spread += [(m[0], m[2]), (m[1], m[3]), (m[2], m[0]), (m[3], m[1])]
        trade += [(m[0], m[1]), (m[1], m[0]), (m[2], m[3]), (m[3], m[2])]
    return everywhere(spread), everywhere(trade)


SPREAD, TRADE = member_pairs()


def send(value, pairs):
    return lax.ppermute(value, AXES, pairs)


def in_vmem(value):
    return pltpu.with_memory_space_constraint(value, pltpu.VMEM)


def payload_kernel(info, front, beside, *refs):
    outs, sems = refs[:-1], refs[-1]

    def copies(source, half):
        made = []
        for at, (delta, out) in enumerate(zip(DELTAS, outs)):
            begin = pl.multiple_of((info[1] + delta) % 4 * SHARE + half * (ROWS // 2), SHARE)
            pivots, rows = source.at[half * DPART : (half + 1) * DPART, :], source.at[pl.ds(begin, SHARE), :]
            made.append(pltpu.make_async_copy(pivots, out.at[0:DPART, :], sems.at[2 * at]))
            made.append(pltpu.make_async_copy(rows, out.at[DPART:, :], sems.at[2 * at + 1]))
        return made

    for half, source in enumerate((front, beside)):
        @pl.when(info[0] == half)
        def _():
            for copy in copies(source, half):
                copy.start()

    for copy in copies(front, 0):
        copy.wait()


def payloads(info, front, beside):
    hbm = pl.BlockSpec(memory_space=pltpu.HBM)
    front = pltpu.with_memory_space_constraint(front, pltpu.HBM)
    return pl.pallas_call(
        payload_kernel,
        out_shape=tuple(pltpu.VMEM((DPART + SHARE, WIDTH), jnp.float32) for _ in DELTAS),
        in_specs=[pl.BlockSpec(memory_space=pltpu.SMEM), hbm, pl.BlockSpec(memory_space=pltpu.VMEM)],
        out_specs=tuple(pl.BlockSpec(memory_space=pltpu.VMEM) for _ in DELTAS),
        scratch_shapes=[pltpu.SemaphoreType.DMA((2 * len(DELTAS),))],
        compiler_params=pltpu.CompilerParams(vmem_limit_bytes=4 << 20),
        name="payloads",
    )(info, front, in_vmem(beside))


def split3(value):
    high = value.astype(jnp.bfloat16)
    rest = value - high.astype(jnp.float32)
    middle = rest.astype(jnp.bfloat16)
    low = (rest - middle.astype(jnp.float32)).astype(jnp.bfloat16)
    return high, middle, low


def stacked_dot(left, right):
    lh, lm, ll = split3(left)
    rh, rm, rl = split3(right)
    lefts = jnp.concatenate([ll, lh, lm, lm, lh, lh], axis=1)
    rights = jnp.concatenate([rh, rl, rm, rh, rm, rh], axis=0)
    return jnp.dot(lefts, rights, preferred_element_type=jnp.float32)


def split2(value):
    high = value.astype(jnp.bfloat16)
    return high, (value - high.astype(jnp.float32)).astype(jnp.bfloat16)


def short_dot(left, right):
    lh, lm = split2(left)
    rh, rm = split2(right)
    lefts = jnp.concatenate([lm, lm, lh, lh], axis=1)
    rights = jnp.concatenate([rm, rh, rm, rh], axis=0)
    return jnp.dot(lefts, rights, preferred_element_type=jnp.float32)


def factor_kernel(info, d_mine, d_other, top, update_out, top_out, f, sem):
    core = info[0]
    kind = jnp.where(info[1] == 0, 0, info[2] + 1)
    sides = (slice(P_SIZE, P_SIZE + WIDTH), slice(0, WIDTH), slice(WIDTH, P_SIZE))
    for half in range(2):
        @pl.when(core == half)
        def _():
            for part in range(2):
                f[half * DPART : (half + 1) * DPART, part * WIDTH : (part + 1) * WIDTH] = d_mine[part]
                f[(1 - half) * DPART : (2 - half) * DPART, part * WIDTH : (part + 1) * WIDTH] = d_other[part]

    f[0:P_SIZE, P_SIZE:] = top[...]
    rows = lax.broadcasted_iota(jnp.int32, (P_SIZE, P_SIZE), 0)
    cols = lax.broadcasted_iota(jnp.int32, (P_SIZE, P_SIZE), 1)
    f[P_SIZE:, 0:P_SIZE] = jnp.where(rows == cols, 1.0, 0.0)
    f[P_SIZE:, P_SIZE:] = jnp.zeros((P_SIZE, WIDTH), jnp.float32)
    total = P_SIZE + WIDTH
    for block in range(P_SIZE // B):
        lo, hi = block * B, block * B + B
        base = lo // WIDTH * WIDTH
        r = lax.broadcasted_iota(jnp.int32, (WIDTH, WIDTH), 0) + base
        c = lax.broadcasted_iota(jnp.int32, (WIDTH, WIDTH), 1) + base
        in_block = (r >= lo) & (r < hi) & (c >= lo) & (c < hi)
        on_diag = in_block & (r == c)
        window = f[base : base + WIDTH, base : base + WIDTH]
        pivot = jnp.where(in_block, window, 0.0)
        diag = jnp.where(on_diag, window, 0.0)
        diag_row = jnp.sum(diag, axis=0, keepdims=True)
        diag_col = jnp.sum(diag, axis=1, keepdims=True)
        inv_row = 1.0 / jnp.where(diag_row == 0.0, 1.0, diag_row)
        inv_col = 1.0 / jnp.where(diag_col == 0.0, 1.0, diag_col)
        inverse = jnp.where(on_diag, 2.0 * inv_row, 0.0) - inv_col * (pivot * inv_row)
        for _ in range(ITERS - 1):
            inverse = 2.0 * inverse - stacked_dot(inverse, stacked_dot(pivot, inverse))
        left_col = hi // WIDTH * WIDTH
        col = lax.broadcasted_iota(jnp.int32, (WIDTH, total - left_col), 1) + left_col
        upper = jnp.where(col >= hi, f[base : base + WIDTH, left_col:], 0.0)
        for first, last, product in ((hi, P_SIZE, stacked_dot), (P_SIZE, 2 * P_SIZE, short_dot)):
            if first == last:
                continue
            window_rows = slice(first, last)
            lower = product(f[window_rows, base : base + WIDTH], inverse)
            f[window_rows, left_col:] = f[window_rows, left_col:] - product(lower, upper)
            lane = lax.broadcasted_iota(jnp.int32, lower.shape, 1) + base
            mine = (lane >= lo) & (lane < hi)
            f[window_rows, base : base + WIDTH] = jnp.where(mine, lower, f[window_rows, base : base + WIDTH])
        if block == P_SIZE // B - 2:
            for case, side in enumerate(sides):
                @pl.when(kind == case)
                def _():
                    pltpu.make_async_copy(f.at[0:P_SIZE, side], top_out, sem).start()

    def finish(update):
        high = update.astype(jnp.bfloat16)
        low = (update - high.astype(jnp.float32)).astype(jnp.bfloat16)
        update_out[...] = jnp.concatenate([high, low], axis=1)

    for case, side in enumerate(sides):
        @pl.when(kind == case)
        def _():
            finish(f[P_SIZE:, side])

    pltpu.make_async_copy(f.at[0:P_SIZE, sides[0]], top_out, sem).wait()


def factor(info, d_mine, d_other, top):
    vmem = pl.BlockSpec(memory_space=pltpu.VMEM)
    return pl.pallas_call(
        factor_kernel,
        out_shape=(pltpu.VMEM((P_SIZE, 2 * WIDTH), jnp.bfloat16), pltpu.HBM((P_SIZE, WIDTH), jnp.float32)),
        in_specs=[pl.BlockSpec(memory_space=pltpu.SMEM), vmem, vmem, vmem],
        out_specs=(vmem, pl.BlockSpec(memory_space=pltpu.HBM)),
        scratch_shapes=[pltpu.VMEM((2 * P_SIZE, P_SIZE + WIDTH), jnp.float32), pltpu.SemaphoreType.DMA],
        compiler_params=pltpu.CompilerParams(vmem_limit_bytes=4 << 20),
        cost_estimate=pl.CostEstimate(flops=9_000_000_000, bytes_accessed=2_000_000, transcendentals=0),
        name="factor",
    )(info, in_vmem(d_mine), in_vmem(d_other), in_vmem(top))


def update_kernel(info, front, *refs):
    out, blocks, top_rows, loads, stores, top_sem = refs[-6:]
    count = blocks.shape[0]
    parts, update, top = refs[:count], refs[count], refs[count + 1]
    top_load = pltpu.make_async_copy(top, top_rows, top_sem)
    has_top = [(info[2 + at] == 0) & (info[1] == 0) for at in range(count)]

    def load(at):
        rows = pl.ds(pl.multiple_of(info[2 + at] * SHARE, SHARE), SHARE)
        return pltpu.make_async_copy(front.at[rows, :], blocks.at[at], loads.at[at])

    def store(at, half):
        begin = pl.multiple_of(info[2 + at] * SHARE + half * P_SIZE, P_SIZE)
        mine = blocks.at[at, half * P_SIZE : (half + 1) * P_SIZE, :]
        return pltpu.make_async_copy(mine, out.at[pl.ds(begin, P_SIZE), :], stores.at[at, half])

    for at in range(count):
        load(at).start()
        pl.when(has_top[at])(top_load.start)
    twice = jnp.concatenate([update[...], update[...]], axis=0)
    for at in range(count):
        for half in range(2):
            rows = slice(half * P_SIZE, (half + 1) * P_SIZE)
            panel = jnp.concatenate([parts[at][0, rows, :], parts[at][1, rows, :]], axis=1)
            high = panel.astype(jnp.bfloat16)
            low = (panel - high.astype(jnp.float32)).astype(jnp.bfloat16)
            both = jnp.dot(jnp.concatenate([high, low], axis=1), twice, preferred_element_type=jnp.float32)
            added = both[:, :WIDTH] + both[:, WIDTH:]
            if half == 0:
                load(at).wait()
            blocks[at, rows, :] = jnp.where(info[0] == 0, blocks[at, rows, :], 0.0) + added
            if half == 0:
                @pl.when(has_top[at])
                def _():
                    top_load.wait()
                    blocks[at, 0:P_SIZE, :] = top_rows[...]

            store(at, half).start()
    for at in range(count):
        for half in range(2):
            store(at, half).wait()


def apply_update(info, front, parts, update, top, done=None):
    vmem, hbm = pl.BlockSpec(memory_space=pltpu.VMEM), pl.BlockSpec(memory_space=pltpu.HBM)
    count = len(parts)
    front = pltpu.with_memory_space_constraint(front, pltpu.HBM)
    return pl.pallas_call(
        update_kernel,
        out_shape=jax.ShapeDtypeStruct((ROWS, WIDTH), jnp.float32),
        in_specs=[pl.BlockSpec(memory_space=pltpu.SMEM), hbm] + [vmem] * (count + 1) + [hbm] * (1 + (done is not None)),
        out_specs=hbm,
        scratch_shapes=[
            pltpu.VMEM((count, SHARE, WIDTH), jnp.float32),
            pltpu.VMEM((P_SIZE, WIDTH), jnp.float32),
            pltpu.SemaphoreType.DMA((count,)),
            pltpu.SemaphoreType.DMA((count, 2)),
            pltpu.SemaphoreType.DMA,
        ],
        input_output_aliases={} if done is None else {count + 4: 0},
        compiler_params=pltpu.CompilerParams(vmem_limit_bytes=4 << 20),
        cost_estimate=pl.CostEstimate(flops=3_000_000_000, bytes_accessed=4_000_000, transcendentals=0),
    )(info, front, *map(in_vmem, parts), in_vmem(update), pltpu.with_memory_space_constraint(top, pltpu.HBM), *([] if done is None else [done]))


def per_device(front):
    row, x, core, z, y = (lax.axis_index(a) for a in AXES)
    mine = coset(z, y)
    panel = (x == 0) & (z == 0) & (y < 2) & (core == 0)
    info = jnp.stack([core, panel.astype(jnp.int32), y, row]).astype(jnp.int32)

    beside = send(front, CORE_SWAP)
    to_up, to_down, to_side, to_self = payloads(jnp.stack([core, mine]).astype(jnp.int32), front, beside)
    up = send(to_up, shift(1, 0))
    down = send(to_down, shift(-1, 0))
    side = send(to_side, SIDE)
    near = y < 2
    held = jnp.where((z == 1) & near, up, jnp.where((z == 3) & near, down, jnp.where(near, to_self, side)))
    held = jnp.where(x == 0, held, send(held, X_SWAP))

    role = member(z, y)
    part = jnp.where(role < 2, held, send(held, SPREAD))
    top_swapped = send(front[:P_SIZE], ROW_SWAP)
    top = jnp.where(row == 0, front[:P_SIZE], top_swapped)
    part, d_part = part[DPART:], part[:DPART]
    other = send(part, TRADE)
    d_part = jnp.where(row == 0, d_part, send(d_part, ROW_SWAP))
    d_traded = send(d_part, TRADE)

    def in_order(a, b):
        first = role % 2 == 0
        return jnp.stack([jnp.where(first, a, b), jnp.where(first, b, a)])

    own = in_order(part, other)
    d_mine = in_order(d_part, d_traded)
    before = send(own, shift(1, 0))
    after = send(own, shift(-1, 0))
    far = send(own, shift(0, 1))
    d_other = send(d_mine, CORE_SWAP)
    own_other = send(own, CORE_SWAP)
    update, top_done = factor(info, d_mine, d_other, top)

    def at(*blocks):
        return jnp.stack([panel.astype(jnp.int32), row, *blocks]).astype(jnp.int32)

    here, there = core * 4, (1 - core) * 4
    earlier, later, middle = (mine + 3) % 4, (mine + 1) % 4, (mine + 2) % 4
    before_other = send(before, CORE_SWAP)
    places = at(mine + here, mine + there, earlier + here)
    out = apply_update(places, front, (own, own_other, before), update, top_done)
    after_other, far_other = send(after, CORE_SWAP), send(far, CORE_SWAP)
    places = at(later + here, middle + here, earlier + there)
    out = apply_update(places, front, (after, far, before_other), update, top_done, out)
    places = at(later + there, middle + there)
    return apply_update(places, front, (after_other, far_other), update, top_done, out)


def solution(mesh):
    wide = jax.sharding.Mesh(mesh.devices.reshape(SHAPE), AXES)
    spec = P("row", ("x", "core", "z", "y"))

    return jax.shard_map(per_device, mesh=wide, in_specs=(spec,), out_specs=spec, check_vma=False)
```

```python
import jax
import jax.numpy as jnp
from jax import lax
from jax.experimental import pallas as pl
from jax.experimental.pallas import tpu as pltpu
from jax.sharding import PartitionSpec as P


B = 64
ITERS = 2
P_SIZE = 256

AXES = ("row", "x", "core", "z", "y")
SHAPE = (2, 2, 2, 4, 4)
ROWS = 4096
WIDTH = 128
SHARE = 512
DELTAS = (1, 3, 2, 0)
LAG = 2
DPART = 128


def place(r, x, c, z, y):
    return (((r * 2 + x) * 2 + c) * 4 + z % 4) * 4 + y % 4


def everywhere(zy_pairs, xs=(0, 1)):
    return [
        (place(r, x, c, *a), place(r, x, c, *b)) for r in range(2) for x in xs for c in range(2) for a, b in zy_pairs
    ]


ALL_ZY = [(z, y) for z in range(4) for y in range(4)]


def shift(dz, dy):
    return everywhere([((z, y), (z + dz, y + dy)) for z, y in ALL_ZY])


ROW_DOWN = [(place(0, x, c, z, y), place(1, x, c, z, y)) for x in range(2) for c in range(2) for z, y in ALL_ZY]
CORE_SWAP = [
    (place(r, x, c, z, y), place(r, x, 1 - c, z, y)) for r in range(2) for x in range(2) for c in range(2) for z, y in ALL_ZY
]
X_SWAP = [
    (place(r, x, c, z, y), place(r, 1 - x, c, z, y)) for r in range(2) for x in range(2) for c in range(2) for z, y in ALL_ZY
]


def coset(z, y):
    return (z + 2 * y) % 4


SIDE = everywhere([((z, y), (z, 3 - y)) for z, y in ALL_ZY])
ROW_SWAP = ROW_DOWN + [(b, a) for a, b in ROW_DOWN]


def member(z, y):
    near = ((y == 0) & (z != 2)) | ((y == 3) & (z == 0))
    far = ((y == 1) & (z != 2)) | ((y == 2) & (z == 0))
    third = ((y == 2) & (z != 0)) | ((y == 1) & (z == 2))
    return 3 - 3 * near - 2 * far - third


def member_pairs():
    spread, trade = [], []
    for c in range(4):
        m = {int(member(z, y)): (z, y) for z, y in ALL_ZY if coset(z, y) == c}
        spread += [(m[0], m[2]), (m[1], m[3]), (m[2], m[0]), (m[3], m[1])]
        trade += [(m[0], m[1]), (m[1], m[0]), (m[2], m[3]), (m[3], m[2])]
    return everywhere(spread), everywhere(trade)


SPREAD, TRADE = member_pairs()


def send(value, pairs):
    return lax.ppermute(value, AXES, pairs)


def in_vmem(value):
    return pltpu.with_memory_space_constraint(value, pltpu.VMEM)


def payload_copies(info, source, half, outs, sems):
    made = []
    for at, (delta, out) in enumerate(zip(DELTAS, outs)):
        begin = pl.multiple_of((info[1] + delta) % 4 * SHARE + half * (ROWS // 2), SHARE)
        pivots, rows = source.at[half * DPART : (half + 1) * DPART, :], source.at[pl.ds(begin, SHARE), :]
        made.append(pltpu.make_async_copy(pivots, out.at[0:DPART, :], sems.at[2 * at]))
        made.append(pltpu.make_async_copy(rows, out.at[DPART:, :], sems.at[2 * at + 1]))
    return made


def kept_kernel(info, front, *refs):
    made = payload_copies(info, front, 0, refs[:-1], refs[-1])
    for copy in made:
        copy.start()
    for copy in made:
        copy.wait()


def taken_kernel(info, beside, *refs):
    made = payload_copies(info, beside, 1, refs[len(DELTAS) : -1], refs[-1])

    @pl.when(info[0] == 1)
    def _():
        for copy in made:
            copy.start()
        for copy in made:
            copy.wait()


def payloads(info, front, beside):
    vmem = pl.BlockSpec(memory_space=pltpu.VMEM)
    smem, hbm = pl.BlockSpec(memory_space=pltpu.SMEM), pl.BlockSpec(memory_space=pltpu.HBM)
    count = len(DELTAS)
    options = dict(
        out_shape=tuple(pltpu.VMEM((DPART + SHARE, WIDTH), jnp.float32) for _ in DELTAS),
        out_specs=(vmem,) * count,
        scratch_shapes=[pltpu.SemaphoreType.DMA((2 * count,))],
        compiler_params=pltpu.CompilerParams(vmem_limit_bytes=4 << 20),
    )
    front = pltpu.with_memory_space_constraint(front, pltpu.HBM)
    kept = pl.pallas_call(kept_kernel, in_specs=[smem, hbm], name="kept", **options)(info, front)
    aliases = {2 + at: at for at in range(count)}
    taken = pl.pallas_call(
        taken_kernel, in_specs=[smem] + [vmem] * (1 + count), input_output_aliases=aliases, name="taken", **options
    )
    return taken(info, in_vmem(beside), *map(in_vmem, kept))


def split3(value):
    high = value.astype(jnp.bfloat16)
    rest = value - high.astype(jnp.float32)
    middle = rest.astype(jnp.bfloat16)
    low = (rest - middle.astype(jnp.float32)).astype(jnp.bfloat16)
    return high, middle, low


def stacked_dot(left, right):
    lh, lm, ll = split3(left)
    rh, rm, rl = split3(right)
    lefts = jnp.concatenate([ll, lh, lm, lm, lh, lh], axis=1)
    rights = jnp.concatenate([rh, rl, rm, rh, rm, rh], axis=0)
    return jnp.dot(lefts, rights, preferred_element_type=jnp.float32)


def split2(value):
    high = value.astype(jnp.bfloat16)
    return high, (value - high.astype(jnp.float32)).astype(jnp.bfloat16)


def short_dot(left, right):
    lh, lm = split2(left)
    rh, rm = split2(right)
    lefts = jnp.concatenate([lm, lm, lh, lh], axis=1)
    rights = jnp.concatenate([rm, rh, rm, rh], axis=0)
    return jnp.dot(lefts, rights, preferred_element_type=jnp.float32)


def factor_kernel(info, d_mine, d_other, top, update_out, top_out, f, sem):
    core = info[0]
    kind = jnp.where(info[1] == 0, 0, info[2] + 1)
    sides = (slice(P_SIZE, P_SIZE + WIDTH), slice(0, WIDTH), slice(WIDTH, P_SIZE))
    for half in range(2):
        @pl.when(core == half)
        def _():
            for part in range(2):
                f[half * DPART : (half + 1) * DPART, part * WIDTH : (part + 1) * WIDTH] = d_mine[part]
                f[(1 - half) * DPART : (2 - half) * DPART, part * WIDTH : (part + 1) * WIDTH] = d_other[part]

    f[0:P_SIZE, P_SIZE:] = top[...]
    rows = lax.broadcasted_iota(jnp.int32, (P_SIZE, P_SIZE), 0)
    cols = lax.broadcasted_iota(jnp.int32, (P_SIZE, P_SIZE), 1)
    f[P_SIZE:, 0:P_SIZE] = jnp.where(rows == cols, 1.0, 0.0)
    f[P_SIZE:, P_SIZE:] = jnp.zeros((P_SIZE, WIDTH), jnp.float32)
    total = P_SIZE + WIDTH
    for block in range(P_SIZE // B):
        lo, hi = block * B, block * B + B
        base = lo // WIDTH * WIDTH
        r = lax.broadcasted_iota(jnp.int32, (WIDTH, WIDTH), 0) + base
        c = lax.broadcasted_iota(jnp.int32, (WIDTH, WIDTH), 1) + base
        in_block = (r >= lo) & (r < hi) & (c >= lo) & (c < hi)
        on_diag = in_block & (r == c)
        window = f[base : base + WIDTH, base : base + WIDTH]
        pivot = jnp.where(in_block, window, 0.0)
        diag = jnp.where(on_diag, window, 0.0)
        diag_row = jnp.sum(diag, axis=0, keepdims=True)
        diag_col = jnp.sum(diag, axis=1, keepdims=True)
        inv_row = 1.0 / jnp.where(diag_row == 0.0, 1.0, diag_row)
        inv_col = 1.0 / jnp.where(diag_col == 0.0, 1.0, diag_col)
        inverse = jnp.where(on_diag, 2.0 * inv_row, 0.0) - inv_col * (pivot * inv_row)
        for _ in range(ITERS - 1):
            inverse = 2.0 * inverse - stacked_dot(inverse, stacked_dot(pivot, inverse))
        left_col = hi // WIDTH * WIDTH
        col = lax.broadcasted_iota(jnp.int32, (WIDTH, total - left_col), 1) + left_col
        upper = jnp.where(col >= hi, f[base : base + WIDTH, left_col:], 0.0)
        for first, last, product in ((hi, P_SIZE, stacked_dot), (P_SIZE, 2 * P_SIZE, short_dot)):
            if first == last:
                continue
            window_rows = slice(first, last)
            lower = product(f[window_rows, base : base + WIDTH], inverse)
            f[window_rows, left_col:] = f[window_rows, left_col:] - product(lower, upper)
            lane = lax.broadcasted_iota(jnp.int32, lower.shape, 1) + base
            mine = (lane >= lo) & (lane < hi)
            f[window_rows, base : base + WIDTH] = jnp.where(mine, lower, f[window_rows, base : base + WIDTH])
        if block == P_SIZE // B - 2:
            for case, side in enumerate(sides):
                @pl.when(kind == case)
                def _():
                    pltpu.make_async_copy(f.at[0:P_SIZE, side], top_out, sem).start()

    def finish(update):
        high = update.astype(jnp.bfloat16)
        low = (update - high.astype(jnp.float32)).astype(jnp.bfloat16)
        update_out[...] = jnp.concatenate([high, low], axis=1)

    for case, side in enumerate(sides):
        @pl.when(kind == case)
        def _():
            finish(f[P_SIZE:, side])

    pltpu.make_async_copy(f.at[0:P_SIZE, sides[0]], top_out, sem).wait()


def factor(info, d_mine, d_other, top):
    vmem = pl.BlockSpec(memory_space=pltpu.VMEM)
    return pl.pallas_call(
        factor_kernel,
        out_shape=(pltpu.VMEM((P_SIZE, 2 * WIDTH), jnp.bfloat16), pltpu.HBM((P_SIZE, WIDTH), jnp.float32)),
        in_specs=[pl.BlockSpec(memory_space=pltpu.SMEM), vmem, vmem, vmem],
        out_specs=(vmem, pl.BlockSpec(memory_space=pltpu.HBM)),
        scratch_shapes=[pltpu.VMEM((2 * P_SIZE, P_SIZE + WIDTH), jnp.float32), pltpu.SemaphoreType.DMA],
        compiler_params=pltpu.CompilerParams(vmem_limit_bytes=4 << 20),
        cost_estimate=pl.CostEstimate(flops=9_000_000_000, bytes_accessed=2_000_000, transcendentals=0),
        name="factor",
    )(info, in_vmem(d_mine), in_vmem(d_other), in_vmem(top))


def update_kernel(info, front, *refs):
    out, blocks, added, top_rows, loads, stores, top_sem = refs[-7:]
    count = blocks.shape[0]
    parts, update, top = refs[:count], refs[count], refs[count + 1]
    top_load = pltpu.make_async_copy(top, top_rows, top_sem)
    has_top = [(info[2 + at] == 0) & (info[1] == 0) for at in range(count)]

    def load(at):
        rows = pl.ds(pl.multiple_of(info[2 + at] * SHARE, SHARE), SHARE)
        return pltpu.make_async_copy(front.at[rows, :], blocks.at[at], loads.at[at])

    def store(at, half):
        begin = pl.multiple_of(info[2 + at] * SHARE + half * P_SIZE, P_SIZE)
        mine = blocks.at[at, half * P_SIZE : (half + 1) * P_SIZE, :]
        return pltpu.make_async_copy(mine, out.at[pl.ds(begin, P_SIZE), :], stores.at[at, half])

    for at in range(count):
        load(at).start()
        pl.when(has_top[at])(top_load.start)
    twice = jnp.concatenate([update[...], update[...]], axis=0)
    halves = [(at, half) for at in range(count) for half in range(2)]

    def multiply(at, half):
        rows = slice(half * P_SIZE, (half + 1) * P_SIZE)
        panel = jnp.concatenate([parts[at][0, rows, :], parts[at][1, rows, :]], axis=1)
        high = panel.astype(jnp.bfloat16)
        low = (panel - high.astype(jnp.float32)).astype(jnp.bfloat16)
        both = jnp.dot(jnp.concatenate([high, low], axis=1), twice, preferred_element_type=jnp.float32)
        added[at, rows, :] = both[:, :WIDTH] + both[:, WIDTH:]

    def finish(at, half):
        rows = slice(half * P_SIZE, (half + 1) * P_SIZE)
        if half == 0:
            load(at).wait()
        blocks[at, rows, :] = jnp.where(info[0] == 0, blocks[at, rows, :], 0.0) + added[at, rows, :]
        if half == 0:
            @pl.when(has_top[at])
            def _():
                top_load.wait()
                blocks[at, 0:P_SIZE, :] = top_rows[...]

        store(at, half).start()

    for turn in range(len(halves) + LAG):
        if turn < len(halves):
            multiply(*halves[turn])
        if turn >= LAG:
            finish(*halves[turn - LAG])
    for at, half in halves:
        store(at, half).wait()


def apply_update(info, front, parts, update, top, done=None):
    vmem, hbm = pl.BlockSpec(memory_space=pltpu.VMEM), pl.BlockSpec(memory_space=pltpu.HBM)
    count = len(parts)
    front = pltpu.with_memory_space_constraint(front, pltpu.HBM)
    return pl.pallas_call(
        update_kernel,
        out_shape=jax.ShapeDtypeStruct((ROWS, WIDTH), jnp.float32),
        in_specs=[pl.BlockSpec(memory_space=pltpu.SMEM), hbm] + [vmem] * (count + 1) + [hbm] * (1 + (done is not None)),
        out_specs=hbm,
        scratch_shapes=[
            pltpu.VMEM((count, SHARE, WIDTH), jnp.float32),
            pltpu.VMEM((count, SHARE, WIDTH), jnp.float32),
            pltpu.VMEM((P_SIZE, WIDTH), jnp.float32),
            pltpu.SemaphoreType.DMA((count,)),
            pltpu.SemaphoreType.DMA((count, 2)),
            pltpu.SemaphoreType.DMA,
        ],
        input_output_aliases={} if done is None else {count + 4: 0},
        compiler_params=pltpu.CompilerParams(vmem_limit_bytes=4 << 20),
        cost_estimate=pl.CostEstimate(flops=3_000_000_000, bytes_accessed=4_000_000, transcendentals=0),
    )(info, front, *map(in_vmem, parts), in_vmem(update), pltpu.with_memory_space_constraint(top, pltpu.HBM), *([] if done is None else [done]))


def per_device(front):
    row, x, core, z, y = (lax.axis_index(a) for a in AXES)
    mine = coset(z, y)
    panel = (x == 0) & (z == 0) & (y < 2) & (core == 0)
    info = jnp.stack([core, panel.astype(jnp.int32), y, row]).astype(jnp.int32)

    beside = send(front, CORE_SWAP)
    to_up, to_down, to_side, to_self = payloads(jnp.stack([core, mine]).astype(jnp.int32), front, beside)
    up = send(to_up, shift(1, 0))
    down = send(to_down, shift(-1, 0))
    side = send(to_side, SIDE)
    near = y < 2
    held = jnp.where((z == 1) & near, up, jnp.where((z == 3) & near, down, jnp.where(near, to_self, side)))
    held = jnp.where(x == 0, held, send(held, X_SWAP))

    role = member(z, y)
    part = jnp.where(role < 2, held, send(held, SPREAD))
    top_swapped = send(front[:P_SIZE], ROW_SWAP)
    top = jnp.where(row == 0, front[:P_SIZE], top_swapped)
    part, d_part = part[DPART:], part[:DPART]
    other = send(part, TRADE)
    d_part = jnp.where(row == 0, d_part, send(d_part, ROW_SWAP))
    d_traded = send(d_part, TRADE)

    def in_order(a, b):
        first = role % 2 == 0
        return jnp.stack([jnp.where(first, a, b), jnp.where(first, b, a)])

    own = in_order(part, other)
    d_mine = in_order(d_part, d_traded)
    before = send(own, shift(1, 0))
    after = send(own, shift(-1, 0))
    far = send(own, shift(0, 1))
    d_other = send(d_mine, CORE_SWAP)
    own_other = send(own, CORE_SWAP)
    update, top_done = factor(info, d_mine, d_other, top)

    def at(*blocks):
        return jnp.stack([panel.astype(jnp.int32), row, *blocks]).astype(jnp.int32)

    here, there = core * 4, (1 - core) * 4
    earlier, later, middle = (mine + 3) % 4, (mine + 1) % 4, (mine + 2) % 4
    before_other = send(before, CORE_SWAP)
    places = at(mine + here, mine + there, earlier + here)
    out = apply_update(places, front, (own, own_other, before), update, top_done)
    after_other, far_other = send(after, CORE_SWAP), send(far, CORE_SWAP)
    places = at(later + here, middle + here, earlier + there)
    out = apply_update(places, front, (after, far, before_other), update, top_done, out)
    places = at(later + there, middle + there)
    return apply_update(places, front, (after_other, far_other), update, top_done, out)


def solution(mesh):
    wide = jax.sharding.Mesh(mesh.devices.reshape(SHAPE), AXES)
    spec = P("row", ("x", "core", "z", "y"))

    return jax.shard_map(per_device, mesh=wide, in_specs=(spec,), out_specs=spec, check_vma=False)
```

```python
import jax
import jax.numpy as jnp
from jax import lax
from jax.experimental import pallas as pl
from jax.experimental.pallas import tpu as pltpu
from jax.sharding import PartitionSpec as P


B = 64
ITERS = 2
P_SIZE = 256

AXES = ("row", "x", "core", "z", "y")
SHAPE = (2, 2, 2, 4, 4)
ROWS = 4096
WIDTH = 128
SHARE = 512
DELTAS = (1, 3, 2, 0)
LAG = 2
DPART = 128


def place(r, x, c, z, y):
    return (((r * 2 + x) * 2 + c) * 4 + z % 4) * 4 + y % 4


def everywhere(zy_pairs, xs=(0, 1)):
    return [
        (place(r, x, c, *a), place(r, x, c, *b)) for r in range(2) for x in xs for c in range(2) for a, b in zy_pairs
    ]


ALL_ZY = [(z, y) for z in range(4) for y in range(4)]


def shift(dz, dy):
    return everywhere([((z, y), (z + dz, y + dy)) for z, y in ALL_ZY])


ROW_DOWN = [(place(0, x, c, z, y), place(1, x, c, z, y)) for x in range(2) for c in range(2) for z, y in ALL_ZY]
CORE_SWAP = [
    (place(r, x, c, z, y), place(r, x, 1 - c, z, y)) for r in range(2) for x in range(2) for c in range(2) for z, y in ALL_ZY
]
X_SWAP = [
    (place(r, x, c, z, y), place(r, 1 - x, c, z, y)) for r in range(2) for x in range(2) for c in range(2) for z, y in ALL_ZY
]


def coset(z, y):
    return (z + 2 * y) % 4


SIDE = everywhere([((z, y), (z, 3 - y)) for z, y in ALL_ZY])
ROW_SWAP = ROW_DOWN + [(b, a) for a, b in ROW_DOWN]


def member(z, y):
    near = ((y == 0) & (z != 2)) | ((y == 3) & (z == 0))
    far = ((y == 1) & (z != 2)) | ((y == 2) & (z == 0))
    third = ((y == 2) & (z != 0)) | ((y == 1) & (z == 2))
    return 3 - 3 * near - 2 * far - third


def member_pairs():
    spread, trade = [], []
    for c in range(4):
        m = {int(member(z, y)): (z, y) for z, y in ALL_ZY if coset(z, y) == c}
        spread += [(m[0], m[2]), (m[1], m[3]), (m[2], m[0]), (m[3], m[1])]
        trade += [(m[0], m[1]), (m[1], m[0]), (m[2], m[3]), (m[3], m[2])]
    return everywhere(spread), everywhere(trade)


SPREAD, TRADE = member_pairs()


def send(value, pairs):
    return lax.ppermute(value, AXES, pairs)


def in_vmem(value):
    return pltpu.with_memory_space_constraint(value, pltpu.VMEM)


def payload_kernel(info, front, beside, *refs):
    outs, sems = refs[:-1], refs[-1]

    def copies(source, half):
        made = []
        for at, (delta, out) in enumerate(zip(DELTAS, outs)):
            begin = pl.multiple_of((info[1] + delta) % 4 * SHARE + half * (ROWS // 2), SHARE)
            pivots, rows = source.at[half * DPART : (half + 1) * DPART, :], source.at[pl.ds(begin, SHARE), :]
            made.append(pltpu.make_async_copy(pivots, out.at[0:DPART, :], sems.at[2 * at]))
            made.append(pltpu.make_async_copy(rows, out.at[DPART:, :], sems.at[2 * at + 1]))
        return made

    for half, source in enumerate((front, beside)):
        @pl.when(info[0] == half)
        def _():
            for copy in copies(source, half):
                copy.start()

    for copy in copies(front, 0):
        copy.wait()


def payloads(info, front, beside):
    hbm = pl.BlockSpec(memory_space=pltpu.HBM)
    front = pltpu.with_memory_space_constraint(front, pltpu.HBM)
    return pl.pallas_call(
        payload_kernel,
        out_shape=tuple(pltpu.VMEM((DPART + SHARE, WIDTH), jnp.float32) for _ in DELTAS),
        in_specs=[pl.BlockSpec(memory_space=pltpu.SMEM), hbm, pl.BlockSpec(memory_space=pltpu.VMEM)],
        out_specs=tuple(pl.BlockSpec(memory_space=pltpu.VMEM) for _ in DELTAS),
        scratch_shapes=[pltpu.SemaphoreType.DMA((2 * len(DELTAS),))],
        compiler_params=pltpu.CompilerParams(vmem_limit_bytes=4 << 20),
        name="payloads",
    )(info, front, in_vmem(beside))


def split3(value):
    high = value.astype(jnp.bfloat16)
    rest = value - high.astype(jnp.float32)
    middle = rest.astype(jnp.bfloat16)
    low = (rest - middle.astype(jnp.float32)).astype(jnp.bfloat16)
    return high, middle, low


def stacked_dot(left, right):
    lh, lm, ll = split3(left)
    rh, rm, rl = split3(right)
    lefts = jnp.concatenate([ll, lh, lm, lm, lh, lh], axis=1)
    rights = jnp.concatenate([rh, rl, rm, rh, rm, rh], axis=0)
    return jnp.dot(lefts, rights, preferred_element_type=jnp.float32)


def split2(value):
    high = value.astype(jnp.bfloat16)
    return high, (value - high.astype(jnp.float32)).astype(jnp.bfloat16)


def short_dot(left, right):
    lh, lm = split2(left)
    rh, rm = split2(right)
    lefts = jnp.concatenate([lm, lm, lh, lh], axis=1)
    rights = jnp.concatenate([rm, rh, rm, rh], axis=0)
    return jnp.dot(lefts, rights, preferred_element_type=jnp.float32)


def factor_kernel(info, d_mine, d_other, top, update_out, top_out, f, sem):
    core = info[0]
    kind = jnp.where(info[1] == 0, 0, info[2] + 1)
    sides = (slice(P_SIZE, P_SIZE + WIDTH), slice(0, WIDTH), slice(WIDTH, P_SIZE))
    for half in range(2):
        @pl.when(core == half)
        def _():
            for part in range(2):
                f[half * DPART : (half + 1) * DPART, part * WIDTH : (part + 1) * WIDTH] = d_mine[part]
                f[(1 - half) * DPART : (2 - half) * DPART, part * WIDTH : (part + 1) * WIDTH] = d_other[part]

    f[0:P_SIZE, P_SIZE:] = top[...]
    rows = lax.broadcasted_iota(jnp.int32, (P_SIZE, P_SIZE), 0)
    cols = lax.broadcasted_iota(jnp.int32, (P_SIZE, P_SIZE), 1)
    f[P_SIZE:, 0:P_SIZE] = jnp.where(rows == cols, 1.0, 0.0)
    f[P_SIZE:, P_SIZE:] = jnp.zeros((P_SIZE, WIDTH), jnp.float32)
    total = P_SIZE + WIDTH
    for block in range(P_SIZE // B):
        lo, hi = block * B, block * B + B
        base = lo // WIDTH * WIDTH
        r = lax.broadcasted_iota(jnp.int32, (WIDTH, WIDTH), 0) + base
        c = lax.broadcasted_iota(jnp.int32, (WIDTH, WIDTH), 1) + base
        in_block = (r >= lo) & (r < hi) & (c >= lo) & (c < hi)
        on_diag = in_block & (r == c)
        window = f[base : base + WIDTH, base : base + WIDTH]
        pivot = jnp.where(in_block, window, 0.0)
        diag = jnp.where(on_diag, window, 0.0)
        diag_row = jnp.sum(diag, axis=0, keepdims=True)
        diag_col = jnp.sum(diag, axis=1, keepdims=True)
        inv_row = 1.0 / jnp.where(diag_row == 0.0, 1.0, diag_row)
        inv_col = 1.0 / jnp.where(diag_col == 0.0, 1.0, diag_col)
        inverse = jnp.where(on_diag, 2.0 * inv_row, 0.0) - inv_col * (pivot * inv_row)
        for _ in range(ITERS - 1):
            inverse = 2.0 * inverse - stacked_dot(inverse, stacked_dot(pivot, inverse))
        left_col = hi // WIDTH * WIDTH
        col = lax.broadcasted_iota(jnp.int32, (WIDTH, total - left_col), 1) + left_col
        upper = jnp.where(col >= hi, f[base : base + WIDTH, left_col:], 0.0)
        for first, last, product in ((hi, P_SIZE, stacked_dot), (P_SIZE, 2 * P_SIZE, short_dot)):
            if first == last:
                continue
            window_rows = slice(first, last)
            lower = product(f[window_rows, base : base + WIDTH], inverse)
            f[window_rows, left_col:] = f[window_rows, left_col:] - product(lower, upper)
            lane = lax.broadcasted_iota(jnp.int32, lower.shape, 1) + base
            mine = (lane >= lo) & (lane < hi)
            f[window_rows, base : base + WIDTH] = jnp.where(mine, lower, f[window_rows, base : base + WIDTH])
        if block == P_SIZE // B - 2:
            for case, side in enumerate(sides):
                @pl.when(kind == case)
                def _():
                    pltpu.make_async_copy(f.at[0:P_SIZE, side], top_out, sem).start()

    def finish(update):
        high = update.astype(jnp.bfloat16)
        low = (update - high.astype(jnp.float32)).astype(jnp.bfloat16)
        update_out[...] = jnp.concatenate([high, low], axis=1)

    for case, side in enumerate(sides):
        @pl.when(kind == case)
        def _():
            finish(f[P_SIZE:, side])

    pltpu.make_async_copy(f.at[0:P_SIZE, sides[0]], top_out, sem).wait()


def factor(info, d_mine, d_other, top):
    vmem = pl.BlockSpec(memory_space=pltpu.VMEM)
    return pl.pallas_call(
        factor_kernel,
        out_shape=(pltpu.VMEM((P_SIZE, 2 * WIDTH), jnp.bfloat16), pltpu.HBM((P_SIZE, WIDTH), jnp.float32)),
        in_specs=[pl.BlockSpec(memory_space=pltpu.SMEM), vmem, vmem, vmem],
        out_specs=(vmem, pl.BlockSpec(memory_space=pltpu.HBM)),
        scratch_shapes=[pltpu.VMEM((2 * P_SIZE, P_SIZE + WIDTH), jnp.float32), pltpu.SemaphoreType.DMA],
        compiler_params=pltpu.CompilerParams(vmem_limit_bytes=4 << 20),
        cost_estimate=pl.CostEstimate(flops=9_000_000_000, bytes_accessed=2_000_000, transcendentals=0),
        name="factor",
    )(info, in_vmem(d_mine), in_vmem(d_other), in_vmem(top))


def update_kernel(info, front, *refs):
    out, blocks, added, top_rows, loads, stores, top_sem = refs[-7:]
    count = blocks.shape[0]
    parts, update, top = refs[:count], refs[count], refs[count + 1]
    top_load = pltpu.make_async_copy(top, top_rows, top_sem)
    has_top = [(info[2 + at] == 0) & (info[1] == 0) for at in range(count)]

    def load(at):
        rows = pl.ds(pl.multiple_of(info[2 + at] * SHARE, SHARE), SHARE)
        return pltpu.make_async_copy(front.at[rows, :], blocks.at[at], loads.at[at])

    def store(at, half):
        begin = pl.multiple_of(info[2 + at] * SHARE + half * P_SIZE, P_SIZE)
        mine = blocks.at[at, half * P_SIZE : (half + 1) * P_SIZE, :]
        return pltpu.make_async_copy(mine, out.at[pl.ds(begin, P_SIZE), :], stores.at[at, half])

    for at in range(count):
        load(at).start()
        pl.when(has_top[at])(top_load.start)
    twice = jnp.concatenate([update[...], update[...]], axis=0)
    halves = [(at, half) for at in range(count) for half in range(2)]

    def multiply(at, half):
        rows = slice(half * P_SIZE, (half + 1) * P_SIZE)
        panel = jnp.concatenate([parts[at][0, rows, :], parts[at][1, rows, :]], axis=1)
        high = panel.astype(jnp.bfloat16)
        low = (panel - high.astype(jnp.float32)).astype(jnp.bfloat16)
        both = jnp.dot(jnp.concatenate([high, low], axis=1), twice, preferred_element_type=jnp.float32)
        added[at, rows, :] = both[:, :WIDTH] + both[:, WIDTH:]

    def finish(at, half):
        rows = slice(half * P_SIZE, (half + 1) * P_SIZE)
        if half == 0:
            load(at).wait()
        blocks[at, rows, :] = jnp.where(info[0] == 0, blocks[at, rows, :], 0.0) + added[at, rows, :]
        if half == 0:
            @pl.when(has_top[at])
            def _():
                top_load.wait()
                blocks[at, 0:P_SIZE, :] = top_rows[...]

        store(at, half).start()

    for turn in range(len(halves) + LAG):
        if turn < len(halves):
            multiply(*halves[turn])
        if turn >= LAG:
            finish(*halves[turn - LAG])
    for at, half in halves:
        store(at, half).wait()


def apply_update(info, front, parts, update, top, done=None):
    vmem, hbm = pl.BlockSpec(memory_space=pltpu.VMEM), pl.BlockSpec(memory_space=pltpu.HBM)
    count = len(parts)
    front = pltpu.with_memory_space_constraint(front, pltpu.HBM)
    return pl.pallas_call(
        update_kernel,
        out_shape=jax.ShapeDtypeStruct((ROWS, WIDTH), jnp.float32),
        in_specs=[pl.BlockSpec(memory_space=pltpu.SMEM), hbm] + [vmem] * (count + 1) + [hbm] * (1 + (done is not None)),
        out_specs=hbm,
        scratch_shapes=[
            pltpu.VMEM((count, SHARE, WIDTH), jnp.float32),
            pltpu.VMEM((count, SHARE, WIDTH), jnp.float32),
            pltpu.VMEM((P_SIZE, WIDTH), jnp.float32),
            pltpu.SemaphoreType.DMA((count,)),
            pltpu.SemaphoreType.DMA((count, 2)),
            pltpu.SemaphoreType.DMA,
        ],
        input_output_aliases={} if done is None else {count + 4: 0},
        compiler_params=pltpu.CompilerParams(vmem_limit_bytes=4 << 20),
        cost_estimate=pl.CostEstimate(flops=3_000_000_000, bytes_accessed=4_000_000, transcendentals=0),
    )(info, front, *map(in_vmem, parts), in_vmem(update), pltpu.with_memory_space_constraint(top, pltpu.HBM), *([] if done is None else [done]))


def per_device(front):
    row, x, core, z, y = (lax.axis_index(a) for a in AXES)
    mine = coset(z, y)
    panel = (x == 0) & (z == 0) & (y < 2) & (core == 0)
    info = jnp.stack([core, panel.astype(jnp.int32), y, row]).astype(jnp.int32)

    beside = send(front, CORE_SWAP)
    to_up, to_down, to_side, to_self = payloads(jnp.stack([core, mine]).astype(jnp.int32), front, beside)
    up = send(to_up, shift(1, 0))
    down = send(to_down, shift(-1, 0))
    side = send(to_side, SIDE)
    near = y < 2
    held = jnp.where((z == 1) & near, up, jnp.where((z == 3) & near, down, jnp.where(near, to_self, side)))
    held = jnp.where(x == 0, held, send(held, X_SWAP))

    role = member(z, y)
    part = jnp.where(role < 2, held, send(held, SPREAD))
    top_swapped = send(front[:P_SIZE], ROW_SWAP)
    top = jnp.where(row == 0, front[:P_SIZE], top_swapped)
    part, d_part = part[DPART:], part[:DPART]
    other = send(part, TRADE)
    d_part = jnp.where(row == 0, d_part, send(d_part, ROW_SWAP))
    d_traded = send(d_part, TRADE)

    def in_order(a, b):
        first = role % 2 == 0
        return jnp.stack([jnp.where(first, a, b), jnp.where(first, b, a)])

    own = in_order(part, other)
    d_mine = in_order(d_part, d_traded)
    before = send(own, shift(1, 0))
    after = send(own, shift(-1, 0))
    far = send(own, shift(0, 1))
    d_other = send(d_mine, CORE_SWAP)
    own_other = send(own, CORE_SWAP)
    update, top_done = factor(info, d_mine, d_other, top)

    def at(*blocks):
        return jnp.stack([panel.astype(jnp.int32), row, *blocks]).astype(jnp.int32)

    here, there = core * 4, (1 - core) * 4
    earlier, later, middle = (mine + 3) % 4, (mine + 1) % 4, (mine + 2) % 4
    before_other = send(before, CORE_SWAP)
    places = at(mine + here, mine + there, earlier + here)
    out = apply_update(places, front, (own, own_other, before), update, top_done)
    after_other, far_other = send(after, CORE_SWAP), send(far, CORE_SWAP)
    places = at(later + here, middle + here, earlier + there)
    out = apply_update(places, front, (after, far, before_other), update, top_done, out)
    places = at(later + there, middle + there)
    return apply_update(places, front, (after_other, far_other), update, top_done, out)


def solution(mesh):
    wide = jax.sharding.Mesh(mesh.devices.reshape(SHAPE), AXES)
    spec = P("row", ("x", "core", "z", "y"))

    return jax.shard_map(per_device, mesh=wide, in_specs=(spec,), out_specs=spec, check_vma=False)
```
